32 devices in a mesh: win: 2 (over x), sta: 16 (over z, y, core).
Axes of the slice: x: 2, y: 2, z: 4, core: 2. Of those that a mesh axis runs over, the one named last changes fastest.
Arguments:
- records: bfloat16 [1024, 16384], P('win', 'sta'), parts along dimension 0, may hold values from -600 to 600
- filter_taps: bfloat16 [129], replicated, may hold values from -0.5 to 0.5
- ref_owner: int32 [4], P('win'), parts along dimension 0, may hold values from 0 to 15
- reference_station_order: int32 [4, 32], P('win'), parts along dimension 0, may hold values from 0 to 31, each once within a row
- pair_valid: int32 [4, 32, 512], P('win', None, 'sta'), parts along dimension 0, may hold values 0 or 1
Outputs:
- correlations: float32 [4, 32, 512, 256], P('win', None, 'sta'), parts along dimension 0
The draws below stay inside these ranges and needn't reach their ends.
There are 2 independent parts, one for each index of `win`. The reference program is written for one: setup_inputs(seed, part) draws one part's arguments, and reference() takes and returns one part's arrays. A program takes and returns all parts, laid end to end along the dimension named above; an argument that names none is the same for every part. Nothing has to cross between parts.
Inputs may be any that keep to these rules, and one draw needn't show every extreme that they name: Each row of reference_station_order is a permutation of 0 .. 31.
All inputs are finite; a program needn't handle non-finite values. No bound on the sum of `pair_valid` on one device may be relied on, other than what follows from the above.
Results may differ from the reference program's by a relative error of at most 0.0073.
Values may be sent and summed in bfloat16 or wider, within the bound.
No kernel may reach another device: no remote copies, remote signals or barrier semaphores. Data moves between devices by JAX's collectives and lax.ppermute only.
A program may use at most 128 MiB of HBM per device.

```python
import math
import jax
import jax.numpy as jnp
from jax import lax

STA_DEV = 32
STATIONS = 512
NFFT = 1024
TRACE_SAMPLES = 16384
TAPS = 129
LAGS = 256
STEPS = 2
N_STA = 16


def draw_records(key, part):
    key_noise = jax.random.fold_in(key, 11)
    key_station = jax.random.fold_in(key, 12)
    pulse_seed_state = jax.random.fold_in(key, 13)
    samples = jnp.clip(jax.random.normal(key_noise, (STATIONS, TRACE_SAMPLES), jnp.float32), -6.0, 6.0)
    station_scale = jnp.exp(jax.random.uniform(key_station, (STATIONS, 1), jnp.float32, 0.0, math.log(10.0)))
    transient_pulses = jnp.exp(jax.random.uniform(pulse_seed_state, (1, TRACE_SAMPLES // 32), jnp.float32, 0.0, math.log(10.0)))
    duration_factor = jnp.repeat(transient_pulses, 32, axis=1)
    return (samples * station_scale * duration_factor).astype(jnp.bfloat16)


def with_ends(values, own_key, least, largest):
    longest = values.shape.index(max(values.shape))
    spots = []
    for shift in (0, 1):
        where = [jax.random.randint(jax.random.fold_in(own_key, axis), (), 0, length) for axis, length in enumerate(values.shape)]
        where[longest] = (where[longest] + shift) % values.shape[longest]
        spots.append(tuple(where))
    return values.at[spots[0]].set(least).at[spots[1]].set(largest)


def centred(key, extent, scale, limit, held_as=jnp.bfloat16):
    result = scale * jax.random.normal(key, extent, jnp.float32)
    return jnp.clip(result, min=-limit, max=limit).astype(held_as)


def setup_inputs(seed: int = 0, part: int = 0) -> dict:
    key_list = jax.random.split(jax.random.key(seed), 6)
    part_splits = jax.random.split(jax.random.fold_in(key_list[5], part), 6)
    records = draw_records(jax.random.fold_in(jax.random.fold_in(key_list[5], part), 71), part)
    filter_taps = centred(key_list[1], (TAPS,), TAPS ** -0.5, 0.5)
    ref_owner = jax.random.randint(part_splits[2], (STEPS,), 0, N_STA).astype(jnp.int32)
    reference_station_order = jax.vmap(lambda own: jax.random.permutation(own, STA_DEV))(jax.random.split(part_splits[3], STEPS)).reshape((STEPS, STA_DEV)).astype(jnp.int32)
    pair_valid = with_ends((jax.random.randint(part_splits[4], (STEPS, STA_DEV, STATIONS), 0, 4) < 3).astype(jnp.int32), jax.random.fold_in(part_splits[4], 1), 0, 1)
    return {"records": records, "filter_taps": filter_taps, "ref_owner": ref_owner, "reference_station_order": reference_station_order, "pair_valid": pair_valid}


def forward_matrix(length):
    time_index = jnp.arange(length, dtype=jnp.int32)[:, None]
    bin_index = jnp.arange(length // 2, dtype=jnp.int32)[None, :]
    angles = (time_index * bin_index % length).astype(jnp.float32) * (2.0 * math.pi / length)
    return jnp.concatenate([jnp.cos(angles), -jnp.sin(angles)], axis=1).astype(jnp.bfloat16)

def inverse_transform_matrix(length, lag_count, segments):
    bin_index = jnp.arange(length // 2, dtype=jnp.int32)[:, None]
    shifts = jnp.arange(lag_count, dtype=jnp.int32)[None, :] - lag_count // 2
    angles = (bin_index * shifts % length).astype(jnp.float32) * (2.0 * math.pi / length)
    factor = 1.0 / math.sqrt(segments * (length // 2))
    return jnp.concatenate([factor * jnp.cos(angles), -factor * jnp.sin(angles)], axis=0).astype(jnp.bfloat16)

def flatten_amplitudes(fourier_coefficients):
    bin_count = fourier_coefficients.shape[-1] // 2
    real_part = fourier_coefficients[..., :bin_count]
    imag_part = fourier_coefficients[..., bin_count:]
    energy = real_part * real_part + imag_part * imag_part
    water_level = lax.optimization_barrier(jnp.mean(energy, axis=-1, keepdims=True))
    factor = lax.rsqrt(energy + water_level + 1e-06)
    return jnp.concatenate([real_part * factor, imag_part * factor], axis=-1).astype(jnp.bfloat16)

def correlate(chosen, resident, inverse):
    bin_count = chosen.shape[-1] // 2
    ref_stack = jnp.stack([chosen[..., :bin_count], chosen[..., bin_count:]], axis=2).astype(jnp.float32)
    direct = jnp.stack([resident[..., :bin_count], resident[..., bin_count:]], axis=2).astype(jnp.float32)
    rotated = jnp.stack([-resident[..., bin_count:], resident[..., :bin_count]], axis=2).astype(jnp.float32)
    real_sum = jnp.einsum('rgcf,sgcf->rsf', ref_stack, direct, precision=lax.Precision.HIGHEST)
    imag_sum = jnp.einsum('rgcf,sgcf->rsf', ref_stack, rotated, precision=lax.Precision.HIGHEST)
    cross = jnp.concatenate([real_sum, imag_sum], axis=-1).astype(jnp.bfloat16)
    ref_count = chosen.shape[0]
    own_count = resident.shape[0]
    lagged = jnp.dot(cross.reshape(ref_count * own_count, 2 * bin_count).astype(jnp.float32), inverse.astype(jnp.float32), precision=lax.Precision.HIGHEST)
    return lagged.reshape(ref_count, own_count, inverse.shape[1])

def reference(records, filter_taps, ref_owner, reference_station_order, pair_valid):
    stations, length = records.shape
    margin = (filter_taps.shape[0] - 1) // 2
    signal = records.astype(jnp.float32)[:, None, :]
    kernel = filter_taps.astype(jnp.float32)[None, None, :]
    filtered_signal = lax.conv_general_dilated(signal, kernel, (1,), [(margin, margin)], precision=lax.Precision.HIGHEST)[:, 0, :].astype(jnp.bfloat16)
    segments = length // NFFT
    fourier_coefficients = jnp.dot(filtered_signal.reshape(stations * segments, NFFT).astype(jnp.float32), forward_matrix(NFFT).astype(jnp.float32), precision=lax.Precision.HIGHEST)
    whitened = flatten_amplitudes(fourier_coefficients.reshape(stations, segments, NFFT))
    inverse = inverse_transform_matrix(NFFT, LAGS, segments)
    resident_blocks = whitened.reshape(N_STA, STA_DEV, segments, NFFT)
    results = []
    for running_total in range(STEPS):
        start_row = (ref_owner[running_total] * STA_DEV).astype(jnp.int32)
        owned = lax.dynamic_slice_in_dim(whitened, start_row, STA_DEV, 0)
        chosen = jnp.take(owned, reference_station_order[running_total].astype(jnp.int32), axis=0)

        def per_block(resident):
            return correlate(chosen, resident, inverse)
        accumulated_sum = lax.map(per_block, resident_blocks)
        merged = jnp.transpose(accumulated_sum, (1, 0, 2, 3)).reshape(STA_DEV, stations, LAGS)
        results.append(merged * pair_valid[running_total].astype(jnp.float32)[:, :, None])
    return jnp.stack(results)
```

```python
import functools
import math

import jax
import jax.numpy as jnp
import numpy as np
from jax import lax
from jax.experimental import pallas as pl
from jax.experimental.pallas import tpu as pltpu
from jax.sharding import PartitionSpec as P

NFFT = 1024
LAGS = 256
LANES = 128
SUB = 8


def forward_matrix(length):
    time_index = np.arange(length)[:, None]
    bin_index = np.arange(length // 2)[None, :]
    angles = (time_index * bin_index % length).astype(np.float32) * np.float32(2.0 * math.pi / length)
    return np.concatenate([np.cos(angles), -np.sin(angles)], axis=1).astype(jnp.bfloat16)


def inverse_transform_matrix(length, lag_count, segments):
    bin_index = np.arange(length // 2)[:, None]
    shifts = np.arange(lag_count)[None, :] - lag_count // 2
    angles = (bin_index * shifts % length).astype(np.float32) * np.float32(2.0 * math.pi / length)
    factor = np.float32(1.0 / math.sqrt(segments * (length // 2)))
    return np.concatenate([factor * np.cos(angles), -factor * np.sin(angles)], axis=0).astype(jnp.bfloat16)


def band_matrix(filter_taps):
    count = filter_taps.shape[0]
    margin = (count - 1) // 2
    height, width = 4 * LANES, 2 * LANES
    offsets = np.arange(height)[:, None] - np.arange(width)[None, :] - LANES + margin
    inside = (offsets >= 0) & (offsets < count)
    column = jnp.zeros((height + 1,), filter_taps.dtype).at[LANES - margin : LANES - margin + count].set(filter_taps)
    flat = jnp.tile(column, width)[: height * width].reshape(width, height)
    return jnp.where(jnp.asarray(inside), flat.T, jnp.zeros((), filter_taps.dtype))


def whiten_body(index_ref, raw_ref, band_ref, forward_ref, out_ref, padded, filtered, *, rows):
    pieces, stations, width = raw_ref.shape
    segments = padded.shape[0]
    bins = NFFT // 2
    edge = jnp.zeros((stations, LANES), raw_ref.dtype)
    padded[0, :, :LANES] = edge
    padded[segments - 1, :, LANES + NFFT :] = edge
    for piece in range(pieces):
        held = raw_ref.at[piece ^ index_ref[0]]
        for part in range(0, width, LANES):
            g, lane = divmod(piece * width + part, NFFT)
            block = held[:, part : part + LANES]
            padded[g, :, LANES + lane : 2 * LANES + lane] = block
            if lane == 0 and g > 0:
                padded[g - 1, :, LANES + NFFT :] = block
            if lane == NFFT - LANES and g < segments - 1:
                padded[g + 1, :, :LANES] = block
    for first in range(0, segments, rows // stations):
        some = slice(first, first + rows // stations)
        for lane in range(0, NFFT, 2 * LANES):
            window = padded[some, :, lane : lane + 4 * LANES].reshape(rows, 4 * LANES)
            filtered[:, lane : lane + 2 * LANES] = jnp.dot(
                window, band_ref[...], preferred_element_type=jnp.float32
            ).astype(jnp.bfloat16)
        spectra = jnp.dot(filtered[...], forward_ref[...], preferred_element_type=jnp.float32)
        real_part, imag_part = spectra[:, :bins], spectra[:, bins:]
        energy = real_part * real_part + imag_part * imag_part
        water_level = jnp.sum(energy, axis=-1, keepdims=True) * (1.0 / bins)
        factor = lax.rsqrt(energy + water_level + 1e-06)
        out_ref[some, :, :bins] = (real_part * factor).astype(jnp.bfloat16).reshape(-1, stations, bins)
        out_ref[some, :, bins:] = (imag_part * factor).astype(jnp.bfloat16).reshape(-1, stations, bins)


def whiten(raw, index, band, forward):
    pieces, stations, width = raw.shape
    segments = pieces * width // NFFT
    rows = min(4, segments) * stations
    return pl.pallas_call(
        functools.partial(whiten_body, rows=rows),
        out_shape=jax.ShapeDtypeStruct((segments, stations, NFFT), jnp.bfloat16),
        in_specs=[pl.BlockSpec(memory_space=pltpu.SMEM)] + [pl.BlockSpec(memory_space=pltpu.VMEM)] * 3,
        out_specs=pl.BlockSpec(memory_space=pltpu.VMEM),
        scratch_shapes=[
            pltpu.VMEM((segments, stations, NFFT + 2 * LANES), jnp.bfloat16),
            pltpu.VMEM((rows, NFFT), jnp.bfloat16),
        ],
        compiler_params=pltpu.CompilerParams(vmem_limit_bytes=40 * 2**20),
        cost_estimate=pl.CostEstimate(
            flops=2 * segments * stations * NFFT * (NFFT + 512), bytes_accessed=2 * raw.size * 2, transcendentals=0
        ),
    )(index, raw, band, forward)


def correlate_body(step_ref, order_ref, valid_ref, own_ref, chosen_ref, inverse_ref, *rest, group, pair, unroll):
    out_ref, own_parts, chosen_parts, cross = rest[-4:]
    segments, stations, width = own_ref.shape
    count = chosen_ref.shape[1]
    bins = width // 2
    tiles = bins // LANES
    step = step_ref[0]
    for g in range(segments):
        for tile in range(tiles):
            real = slice(tile * LANES, (tile + 1) * LANES)
            imag = slice(bins + tile * LANES, bins + (tile + 1) * LANES)
            c, d = own_ref[g, :, real].astype(jnp.float32), own_ref[g, :, imag].astype(jnp.float32)
            own_parts[0, tile, g], own_parts[1, tile, g], own_parts[2, tile, g] = c, c + d, c - d
            a, b = chosen_ref[g, :, real].astype(jnp.float32), chosen_ref[g, :, imag].astype(jnp.float32)
            where = pl.ds(g * count, count)
            chosen_parts[0, tile, where], chosen_parts[1, tile, where], chosen_parts[2, tile, where] = a + b, a, b
    square = (stations, stations)
    diagonal = lax.broadcasted_iota(jnp.int32, square, 0) == lax.broadcasted_iota(jnp.int32, square, 1)

    def some_rows(q, _):
        def products(turn, _):
            tile = lax.rem(turn, tiles)
            first = lax.div(turn, tiles) * pair
            picks = [order_ref[step, q * group + first + j] for j in range(pair)]

            def add_segment(g, sums):
                own = [own_parts[n, tile, g].reshape(stations // SUB, SUB, LANES) for n in range(3)]
                return tuple(
                    sums[3 * j + n] + chosen_parts[n, tile, pl.ds(g * count + pick, SUB, stride=0), :][None] * own[n]
                    for j, pick in enumerate(picks)
                    for n in range(3)
                )

            zero = jnp.zeros((stations // SUB, SUB, LANES), jnp.float32)
            sums = lax.fori_loop(0, segments, add_segment, (zero,) * (3 * pair), unroll=unroll)
            for j in range(pair):
                whole, real, imag = [s.reshape(stations, LANES) for s in sums[3 * j : 3 * j + 3]]
                where = pl.ds(pl.multiple_of((first + j) * stations, stations), stations)
                lanes = pl.multiple_of(tile * LANES, LANES)
                cross[where, pl.ds(lanes, LANES)] = (whole - imag).astype(jnp.bfloat16)
                cross[where, pl.ds(bins + lanes, LANES)] = (whole - real).astype(jnp.bfloat16)
            return 0

        lax.fori_loop(0, group // pair * tiles, products, 0)
        lagged = jnp.dot(cross[...], inverse_ref[...], preferred_element_type=jnp.float32)
        valid = valid_ref[0, pl.ds(pl.multiple_of(q * group, group), group), :].astype(jnp.float32)
        for j in range(group):
            kept = jnp.sum(
                jnp.where(diagonal, jnp.broadcast_to(valid[j : j + 1, :], square), 0.0), axis=1, keepdims=True
            )
            out_ref[0, q * group + j] = lagged[j * stations : (j + 1) * stations] * kept
        return 0

    lax.fori_loop(0, count // group, some_rows, 0)


def correlate(step, order, valid, own, chosen, inverse, earlier=None):
    segments, stations, width = own.shape
    count = chosen.shape[1]
    steps = order.shape[0]
    lags = inverse.shape[1]
    group = SUB
    whole = lambda *shape: pl.BlockSpec(shape, lambda i, s, o: (0,) * len(shape))
    one_step = lambda *shape: pl.BlockSpec((1,) + shape, lambda i, s, o: (s[0],) + (0,) * len(shape))
    extra, aliases = ([], {}) if earlier is None else ([earlier], {6: 0})
    return pl.pallas_call(
        functools.partial(correlate_body, group=group, pair=2, unroll=8),
        out_shape=jax.ShapeDtypeStruct((steps, count, stations, lags), jnp.float32),
        grid_spec=pltpu.PrefetchScalarGridSpec(
            num_scalar_prefetch=2,
            grid=(1,),
            in_specs=[
                one_step(count, stations),
                whole(*own.shape),
                whole(*chosen.shape),
                whole(*inverse.shape),
            ]
            + [pl.BlockSpec(memory_space=pl.ANY)] * len(extra),
            out_specs=one_step(count, stations, lags),
            scratch_shapes=[
                pltpu.VMEM((3, width // 2 // LANES, segments, stations, LANES), jnp.float32),
                pltpu.VMEM((3, width // 2 // LANES, segments * count, LANES), jnp.float32),
                pltpu.VMEM((group * stations, width), jnp.bfloat16),
            ],
        ),
        input_output_aliases=aliases,
        compiler_params=pltpu.CompilerParams(vmem_limit_bytes=40 * 2**20),
        cost_estimate=pl.CostEstimate(
            flops=40 * 10**9, bytes_accessed=own.size * 2 + chosen.size * 2 + count * stations * lags * 4, transcendentals=0
        ),
    )(step, order, valid, own, chosen, inverse, *extra)


def swap(block, axis, distance):
    count = lax.axis_size(axis)
    return lax.ppermute(block, axis, [(i, i ^ distance) for i in range(count)])


def local(records, filter_taps, ref_owner, reference_station_order, pair_valid):
    axis = "sta"
    devices = lax.axis_size(axis)
    index = lax.axis_index(axis).astype(jnp.int32)
    steps = ref_owner.shape[0]
    stations = records.shape[0] // devices
    width = records.shape[1]

    wanted = jnp.stack(
        [lax.dynamic_slice_in_dim(records, ref_owner[k] * stations, stations, 0) for k in range(steps)]
    )
    held = wanted[None]
    distance = devices
    while distance > 2:
        radix = 4 if distance >= 8 else 2
        distance //= radix
        held = jnp.concatenate([held] + [swap(held, axis, j * distance) for j in range(1, radix)], axis=0) if (
            distance * radix == devices
        ) else jnp.stack([held] + [swap(held, axis, j * distance) for j in range(1, radix)], axis=1).reshape(
            (-1,) + held.shape[1:]
        )
    mine = lax.rem(index, 2)
    kept = lax.dynamic_index_in_dim(held, mine, 1, keepdims=False)
    given = lax.dynamic_index_in_dim(held, 1 - mine, 1, keepdims=False)
    pieces = jnp.stack([kept, swap(given, axis, 1)], axis=1).reshape(devices, stations, width)

    rows = lax.all_to_all(records.reshape(devices, stations, width), axis, split_axis=0, concat_axis=0)

    band = band_matrix(filter_taps)
    forward = jnp.asarray(forward_matrix(NFFT))
    inverse = jnp.asarray(inverse_transform_matrix(NFFT, LAGS, devices * width // NFFT))
    first = whiten(pieces, index[None], band, forward)
    second = swap(first, axis, 1)
    own = whiten(rows, jnp.zeros((1,), jnp.int32), band, forward)
    order = reference_station_order
    done = correlate(mine[None], order, pair_valid, own, first, inverse)
    return correlate(1 - mine[None], order, pair_valid, own, second, inverse, done)


def solution(mesh):
    placed = (P("win", "sta"), P(), P("win"), P("win", None), P("win", None, "sta"))
    return jax.shard_map(
        local, mesh=mesh, in_specs=placed, out_specs=P("win", None, "sta", None), check_vma=False
    )
```

```python
import functools
import math

import jax
import jax.numpy as jnp
import numpy as np
from jax import lax
from jax.experimental import pallas as pl
from jax.experimental.pallas import tpu as pltpu
from jax.sharding import PartitionSpec as P

NFFT = 1024
LAGS = 256
LANES = 128
SUB = 8


def forward_matrix(length):
    time_index = np.arange(length)[:, None]
    bin_index = np.arange(length // 2)[None, :]
    angles = (time_index * bin_index % length).astype(np.float32) * np.float32(2.0 * math.pi / length)
    return np.concatenate([np.cos(angles), -np.sin(angles)], axis=1).astype(jnp.bfloat16)


def inverse_transform_matrix(length, lag_count, segments):
    bin_index = np.arange(length // 2)[:, None]
    shifts = np.arange(lag_count)[None, :] - lag_count // 2
    angles = (bin_index * shifts % length).astype(np.float32) * np.float32(2.0 * math.pi / length)
    factor = np.float32(1.0 / math.sqrt(segments * (length // 2)))
    return np.concatenate([factor * np.cos(angles), -factor * np.sin(angles)], axis=0).astype(jnp.bfloat16)


def band_matrix(filter_taps):
    count = filter_taps.shape[0]
    margin = (count - 1) // 2
    height, width = 4 * LANES, 2 * LANES
    offsets = np.arange(height)[:, None] - np.arange(width)[None, :] - LANES + margin
    inside = (offsets >= 0) & (offsets < count)
    column = jnp.zeros((height + 1,), filter_taps.dtype).at[LANES - margin : LANES - margin + count].set(filter_taps)
    flat = jnp.tile(column, width)[: height * width].reshape(width, height)
    return jnp.where(jnp.asarray(inside), flat.T, jnp.zeros((), filter_taps.dtype))


def whiten_body(index_ref, *rest, pieces, rows):
    band_ref, forward_ref, out_ref, padded, filtered = rest[-5:]
    raw_refs = rest[:-5] if len(rest) > 6 else [rest[0].at[piece] for piece in range(pieces)]
    stations = padded.shape[1]
    width = raw_refs[0].shape[-1]
    tiles = NFFT // LANES
    parts = width // LANES
    segments = out_ref.shape[0]
    bins = NFFT // 2
    edge = jnp.zeros((stations, LANES), padded.dtype)
    padded[0] = edge
    padded[segments * tiles + 1] = edge
    for piece in range(pieces):
        place = 1 + (index_ref[0] ^ piece) * parts
        held = raw_refs[piece]
        lead = len(held.shape) == 3
        for part in range(parts):
            lanes = slice(part * LANES, (part + 1) * LANES)
            if lead:
                padded[place + part] = held[:, :, lanes].reshape(stations, LANES)
            else:
                padded[place + part] = held[:, lanes]
    for first in range(0, segments, rows // stations):
        some = range(first, first + rows // stations)
        for tile in range(0, tiles, 2):
            window = jnp.concatenate(
                [jnp.concatenate([padded[g * tiles + tile + i] for g in some], axis=0) for i in range(4)], axis=1
            )
            filtered[:, tile * LANES : (tile + 2) * LANES] = jnp.dot(
                window, band_ref[...], preferred_element_type=jnp.float32
            ).astype(jnp.bfloat16)
        spectra = jnp.dot(filtered[...], forward_ref[...], preferred_element_type=jnp.float32)
        real_part, imag_part = spectra[:, :bins], spectra[:, bins:]
        energy = real_part * real_part + imag_part * imag_part
        water_level = jnp.sum(energy, axis=-1, keepdims=True) * (1.0 / bins)
        factor = lax.rsqrt(energy + water_level + 1e-06)
        some = slice(first, first + rows // stations)
        out_ref[some, :, :bins] = (real_part * factor).astype(jnp.bfloat16).reshape(-1, stations, bins)
        out_ref[some, :, bins:] = (imag_part * factor).astype(jnp.bfloat16).reshape(-1, stations, bins)


def whiten(raw, index, band, forward, rows=128):
    pieces = len(raw)
    width = raw[0].shape[-1]
    stations = math.prod(raw[0].shape[:-1])
    segments = pieces * width // NFFT
    operands = raw if isinstance(raw, list) else [raw]
    return pl.pallas_call(
        functools.partial(whiten_body, pieces=pieces, rows=rows),
        out_shape=jax.ShapeDtypeStruct((segments, stations, NFFT), jnp.bfloat16),
        in_specs=[pl.BlockSpec(memory_space=pltpu.SMEM)] + [pl.BlockSpec(memory_space=pltpu.VMEM)] * (len(operands) + 2),
        out_specs=pl.BlockSpec(memory_space=pltpu.VMEM),
        scratch_shapes=[
            pltpu.VMEM((segments * NFFT // LANES + 2, stations, LANES), jnp.bfloat16),
            pltpu.VMEM((rows, NFFT), jnp.bfloat16),
        ],
        compiler_params=pltpu.CompilerParams(vmem_limit_bytes=24 * 2**20),
        cost_estimate=pl.CostEstimate(
            flops=2 * segments * stations * NFFT * (NFFT + 512),
            bytes_accessed=2 * segments * stations * NFFT * 2,
            transcendentals=0,
        ),
    )(index, *operands, band, forward)


def correlate_body(order_ref, valid_ref, own_ref, chosen_ref, inverse_ref, *rest, group, pair, unroll):
    out_ref, own_parts, chosen_parts, cross = rest[-4:]
    segments, stations, width = own_ref.shape
    steps, block = order_ref.shape
    count = steps * block
    bins = width // 2
    tiles = bins // LANES
    for g in range(segments):
        for tile in range(tiles):
            real = slice(tile * LANES, (tile + 1) * LANES)
            imag = slice(bins + tile * LANES, bins + (tile + 1) * LANES)
            c, d = own_ref[g, :, real].astype(jnp.float32), own_ref[g, :, imag].astype(jnp.float32)
            own_parts[0, tile, g], own_parts[1, tile, g], own_parts[2, tile, g] = c, c + d, c - d
            a, b = chosen_ref[g, :, real].astype(jnp.float32), chosen_ref[g, :, imag].astype(jnp.float32)
            where = pl.ds(g * count, count)
            chosen_parts[0, tile, where], chosen_parts[1, tile, where], chosen_parts[2, tile, where] = a + b, a, b
    square = (stations, stations)
    diagonal = lax.broadcasted_iota(jnp.int32, square, 0) == lax.broadcasted_iota(jnp.int32, square, 1)

    def some_rows(q, _):
        step = lax.div(q, block // group)
        start = lax.rem(q, block // group) * group

        def products(turn, _):
            tile = lax.rem(turn, tiles)
            first = lax.div(turn, tiles) * pair
            picks = [step * block + order_ref[step, start + first + j] for j in range(pair)]

            def add_segment(g, sums):
                own = [own_parts[n, tile, g].reshape(stations // SUB, SUB, LANES) for n in range(3)]
                return tuple(
                    sums[3 * j + n] + chosen_parts[n, tile, pl.ds(g * count + pick, SUB, stride=0), :][None] * own[n]
                    for j, pick in enumerate(picks)
                    for n in range(3)
                )

            zero = jnp.zeros((stations // SUB, SUB, LANES), jnp.float32)
            sums = lax.fori_loop(0, segments, add_segment, (zero,) * (3 * pair), unroll=unroll)
            for j in range(pair):
                whole, real, imag = [s.reshape(stations, LANES) for s in sums[3 * j : 3 * j + 3]]
                where = pl.ds(pl.multiple_of((first + j) * stations, stations), stations)
                lanes = pl.multiple_of(tile * LANES, LANES)
                cross[where, pl.ds(lanes, LANES)] = (whole - imag).astype(jnp.bfloat16)
                cross[where, pl.ds(bins + lanes, LANES)] = (whole - real).astype(jnp.bfloat16)
            return 0

        lax.fori_loop(0, group // pair * tiles, products, 0)
        lagged = jnp.dot(cross[...], inverse_ref[...], preferred_element_type=jnp.float32)
        valid = valid_ref[step, pl.ds(pl.multiple_of(start, group), group), :].astype(jnp.float32)
        for j in range(group):
            kept = jnp.sum(
                jnp.where(diagonal, jnp.broadcast_to(valid[j : j + 1, :], square), 0.0), axis=1, keepdims=True
            )
            out_ref[step, start + j] = lagged[j * stations : (j + 1) * stations] * kept
        return 0

    lax.fori_loop(0, count // group, some_rows, 0)


def correlate(part, parts, order, valid, own, chosen, inverse, earlier=None):
    segments, stations, width = own.shape
    steps, block = order.shape
    count = steps * block
    lags = inverse.shape[1]
    group = 2 * SUB
    whole = lambda *shape: pl.BlockSpec(shape, lambda i, o: (0,) * len(shape))
    extra, aliases = ([], {}) if earlier is None else ([earlier], {5: 0})
    return pl.pallas_call(
        functools.partial(correlate_body, group=group, pair=4, unroll=8),
        out_shape=jax.ShapeDtypeStruct((steps, block, parts * stations, lags), jnp.float32),
        grid_spec=pltpu.PrefetchScalarGridSpec(
            num_scalar_prefetch=1,
            grid=(1,),
            in_specs=[
                whole(steps, block, stations),
                whole(*own.shape),
                whole(*chosen.shape),
                whole(*inverse.shape),
            ]
            + [pl.BlockSpec(memory_space=pl.ANY)] * len(extra),
            out_specs=pl.BlockSpec((steps, block, stations, lags), lambda i, o: (0, 0, part, 0)),
            scratch_shapes=[
                pltpu.VMEM((3, width // 2 // LANES, segments, stations, LANES), jnp.float32),
                pltpu.VMEM((3, width // 2 // LANES, segments * count, LANES), jnp.float32),
                pltpu.VMEM((group * stations, width), jnp.bfloat16),
            ],
        ),
        input_output_aliases=aliases,
        compiler_params=pltpu.CompilerParams(vmem_limit_bytes=24 * 2**20),
        cost_estimate=pl.CostEstimate(
            flops=10**10,
            bytes_accessed=own.size * 2 + chosen.size * 2 + count * stations * lags * 4,
            transcendentals=0,
        ),
    )(order, valid, own, chosen, inverse, *extra)


def swap(block, axis, distance):
    count = lax.axis_size(axis)
    return lax.ppermute(block, axis, [(i, i ^ distance) for i in range(count)])


def local(records, filter_taps, ref_owner, reference_station_order, pair_valid):
    axis = "sta"
    devices = lax.axis_size(axis)
    index = lax.axis_index(axis).astype(jnp.int32)
    steps = ref_owner.shape[0]
    stations = records.shape[0] // devices
    width = records.shape[1]

    wanted = jnp.stack(
        [lax.dynamic_slice_in_dim(records, ref_owner[k] * stations, stations, 0) for k in range(steps)]
    )
    pieces = {0: wanted}
    distance = devices
    while distance > 1:
        radix = 4 if distance >= 16 else 2
        distance //= radix
        pieces |= {o | j * distance: swap(p, axis, j * distance) for o, p in pieces.items() for j in range(1, radix)}
    pieces = [pieces[o] for o in range(devices)]

    parts = 2
    grouped = records.reshape(devices, parts, stations // parts, width)
    resident = [lax.all_to_all(grouped[:, p], axis, split_axis=0, concat_axis=0) for p in range(parts)]

    band = band_matrix(filter_taps)
    forward = jnp.asarray(forward_matrix(NFFT))
    inverse = jnp.asarray(inverse_transform_matrix(NFFT, LAGS, devices * width // NFFT))
    chosen = whiten(pieces, index[None], band, forward)
    zero = jnp.zeros((1,), jnp.int32)
    result = None
    for p in range(parts):
        own = whiten(resident[p], zero, band, forward)
        valid = pair_valid[:, :, p * stations // parts : (p + 1) * stations // parts]
        result = correlate(p, parts, reference_station_order, valid, own, chosen, inverse, result)
    return result


def solution(mesh):
    placed = (P("win", "sta"), P(), P("win"), P("win", None), P("win", None, "sta"))
    return jax.shard_map(
        local, mesh=mesh, in_specs=placed, out_specs=P("win", None, "sta", None), check_vma=False
    )
```

```python
import functools
import math

import jax
import jax.numpy as jnp
import numpy as np
from jax import lax
from jax.experimental import pallas as pl
from jax.experimental.pallas import tpu as pltpu
from jax.sharding import PartitionSpec as P


NFFT = 1024
LAGS = 256
LANES = 128
SUB = 8


def forward_matrix(length):
    time_index = np.arange(length)[:, None]
    bin_index = np.arange(length // 2)[None, :]
    angles = (time_index * bin_index % length).astype(np.float32) * np.float32(2.0 * math.pi / length)
    return np.concatenate([np.cos(angles), -np.sin(angles)], axis=1).astype(jnp.bfloat16)


def inverse_transform_matrix(length, lag_count, segments):
    bin_index = np.arange(length // 2)[:, None]
    shifts = np.arange(lag_count)[None, :] - lag_count // 2
    angles = (bin_index * shifts % length).astype(np.float32) * np.float32(2.0 * math.pi / length)
    factor = np.float32(1.0 / math.sqrt(segments * (length // 2)))
    return np.concatenate([factor * np.cos(angles), -factor * np.sin(angles)], axis=0).astype(jnp.bfloat16)


def pick_body(owner_ref, records_ref, wanted_ref, *rest):
    halves, sems = rest[:-1], rest[-1]
    copies = [
        pltpu.make_async_copy(records_ref.at[owner_ref[k]], wanted_ref.at[k], sems.at[k])
        for k in range(wanted_ref.shape[0])
    ]
    for p, half in enumerate(halves):
        copies.append(pltpu.make_async_copy(records_ref.at[:, p], half, sems.at[len(copies)]))
    for copy in copies:
        copy.start()
    for copy in copies:
        copy.wait()


def pick(owner, records):
    devices, parts, some, width = records.shape
    steps = owner.shape[0]
    vmem = pl.BlockSpec(memory_space=pltpu.VMEM)
    return pl.pallas_call(
        pick_body,
        out_shape=[jax.ShapeDtypeStruct((steps, parts, some, width), records.dtype)]
        + [jax.ShapeDtypeStruct((devices, some, width), records.dtype)] * parts,
        in_specs=[pl.BlockSpec(memory_space=pltpu.SMEM), pl.BlockSpec(memory_space=pltpu.HBM)],
        out_specs=[vmem] * (1 + parts),
        scratch_shapes=[pltpu.SemaphoreType.DMA((steps + parts,))],
        compiler_params=pltpu.CompilerParams(vmem_limit_bytes=8 * 2**20),
    )(owner, records)


def band_body(row_ref, out_ref):
    width, height = 2 * LANES, 4 * LANES
    rows = jnp.broadcast_to(row_ref[...], (width, height))
    out_ref[...] = pltpu.roll(rows, 0, 1, stride=1, stride_axis=0).T.astype(out_ref.dtype)


def band_matrix(filter_taps):
    count = filter_taps.shape[0]
    before = LANES - (count - 1) // 2
    row = jnp.pad(filter_taps.astype(jnp.float32), (before, 4 * LANES - before - count))[None]
    return pl.pallas_call(
        band_body,
        out_shape=jax.ShapeDtypeStruct((4 * LANES, 2 * LANES), filter_taps.dtype),
        in_specs=[pl.BlockSpec(memory_space=pltpu.VMEM)],
        out_specs=pl.BlockSpec(memory_space=pltpu.VMEM),
        compiler_params=pltpu.CompilerParams(vmem_limit_bytes=4 * 2**20),
    )(row)


def whiten_body(index_ref, *rest, pieces, rows):
    band_ref, forward_ref, out_ref, padded, filtered = rest[-5:]
    raw_refs = rest[:-5] if len(rest) > 6 else [rest[0].at[piece] for piece in range(pieces)]
    stations = padded.shape[1]
    width = raw_refs[0].shape[-1]
    tiles = NFFT // LANES
    parts = width // LANES
    segments = out_ref.shape[0]
    bins = NFFT // 2
    edge = jnp.zeros((stations, LANES), padded.dtype)
    padded[0] = edge
    padded[segments * tiles + 1] = edge
    for piece in range(pieces):
        place = 1 + (index_ref[0] ^ piece) * parts
        held = raw_refs[piece]
        lead = len(held.shape) > 2
        for part in range(parts):
            lanes = slice(part * LANES, (part + 1) * LANES)
            if lead:
                padded[place + part] = held[..., lanes].reshape(stations, LANES)
            else:
                padded[place + part] = held[:, lanes]
    for first in range(0, segments, rows // stations):
        some = range(first, first + rows // stations)
        for tile in range(0, tiles, 2):
            window = jnp.concatenate(
                [jnp.concatenate([padded[g * tiles + tile + i] for g in some], axis=0) for i in range(4)], axis=1
            )
            filtered[:, tile * LANES : (tile + 2) * LANES] = jnp.dot(
                window, band_ref[...], preferred_element_type=jnp.float32
            ).astype(jnp.bfloat16)
        spectra = jnp.dot(filtered[...], forward_ref[...], preferred_element_type=jnp.float32)
        real_part, imag_part = spectra[:, :bins], spectra[:, bins:]
        energy = real_part * real_part + imag_part * imag_part
        water_level = jnp.sum(energy, axis=-1, keepdims=True) * (1.0 / bins)
        factor = lax.rsqrt(energy + water_level + 1e-06)
        some = slice(first, first + rows // stations)
        out_ref[some, :, :bins] = (real_part * factor).astype(jnp.bfloat16).reshape(-1, stations, bins)
        out_ref[some, :, bins:] = (imag_part * factor).astype(jnp.bfloat16).reshape(-1, stations, bins)


def whiten(raw, index, band, forward, rows=128):
    pieces = len(raw)
    width = raw[0].shape[-1]
    stations = math.prod(raw[0].shape[:-1])
    segments = pieces * width // NFFT
    operands = raw if isinstance(raw, list) else [raw]
    return pl.pallas_call(
        functools.partial(whiten_body, pieces=pieces, rows=rows),
        out_shape=jax.ShapeDtypeStruct((segments, stations, NFFT), jnp.bfloat16),
        in_specs=[pl.BlockSpec(memory_space=pltpu.SMEM)] + [pl.BlockSpec(memory_space=pltpu.VMEM)] * (len(operands) + 2),
        out_specs=pl.BlockSpec(memory_space=pltpu.VMEM),
        scratch_shapes=[
            pltpu.VMEM((segments * NFFT // LANES + 2, stations, LANES), jnp.bfloat16),
            pltpu.VMEM((rows, NFFT), jnp.bfloat16),
        ],
        compiler_params=pltpu.CompilerParams(vmem_limit_bytes=10 * 2**20),
        cost_estimate=pl.CostEstimate(
            flops=2 * segments * stations * NFFT * (NFFT + 512),
            bytes_accessed=2 * segments * stations * NFFT * 2,
            transcendentals=0,
        ),
    )(index, *operands, band, forward)


def correlate_body(order_ref, valid_ref, own_ref, chosen_ref, inverse_ref, *rest, part, group, pair):
    out_ref, own_parts, chosen_parts, cross, ready, sems = rest[-6:]
    segments, stations, width = own_ref.shape
    steps, block = order_ref.shape
    count = steps * block
    bins = width // 2
    tiles = bins // LANES

    def prepare(g, _):
        where = pl.ds(pl.multiple_of(g * count, count), count)
        for tile in range(tiles):
            real = slice(tile * LANES, (tile + 1) * LANES)
            imag = slice(bins + tile * LANES, bins + (tile + 1) * LANES)
            c, d = own_ref[g, :, real].astype(jnp.float32), own_ref[g, :, imag].astype(jnp.float32)
            own_parts[0, tile, g], own_parts[1, tile, g], own_parts[2, tile, g] = c, c + d, c - d
            a, b = chosen_ref[g, :, real].astype(jnp.float32), chosen_ref[g, :, imag].astype(jnp.float32)
            chosen_parts[0, tile, where], chosen_parts[1, tile, where], chosen_parts[2, tile, where] = a + b, a, b
        return 0

    lax.fori_loop(0, segments, prepare, 0, unroll=2)
    square = (stations, stations)
    diagonal = lax.broadcasted_iota(jnp.int32, square, 0) == lax.broadcasted_iota(jnp.int32, square, 1)

    def place(q):
        step = lax.div(q, block // group)
        start = pl.multiple_of(lax.rem(q, block // group) * group, group)
        return step, start

    def send(q):
        step, start = place(q)
        slot = lax.rem(q, 2)
        where = out_ref.at[step, pl.ds(start, group), pl.ds(part * stations, stations), :]
        return pltpu.make_async_copy(ready.at[slot], where, sems.at[slot])

    def some_rows(q, _):
        step, start = place(q)

        def products(turn, _):
            tile = lax.rem(turn, tiles)
            first = lax.div(turn, tiles) * pair
            picks = [step * block + order_ref[step, start + first + j] for j in range(pair)]
            sums = None
            for g in range(segments):
                own = [own_parts[n, tile, g].reshape(stations // SUB, SUB, LANES) for n in range(3)]
                terms = [
                    chosen_parts[n, tile, pl.ds(g * count + pick, SUB, stride=0), :][None] * own[n]
                    for pick in picks
                    for n in range(3)
                ]
                sums = terms if sums is None else [x + y for x, y in zip(sums, terms)]
            for j in range(pair):
                whole, real, imag = [s.reshape(stations, LANES) for s in sums[3 * j : 3 * j + 3]]
                where = pl.ds(pl.multiple_of((first + j) * stations, stations), stations)
                lanes = pl.multiple_of(tile * LANES, LANES)
                cross[where, pl.ds(lanes, LANES)] = (whole - imag).astype(jnp.bfloat16)
                cross[where, pl.ds(bins + lanes, LANES)] = (whole - real).astype(jnp.bfloat16)
            return 0

        lax.fori_loop(0, group // pair * tiles, products, 0)
        lagged = jnp.dot(cross[...], inverse_ref[...], preferred_element_type=jnp.float32)
        valid = valid_ref[step, pl.ds(start, group), :].astype(jnp.float32)

        @pl.when(q >= 2)
        def _():
            send(q - 2).wait()

        slot = lax.rem(q, 2)
        for j in range(group):
            row = valid[j : j + 1, part * stations : (part + 1) * stations]
            kept = jnp.sum(jnp.where(diagonal, jnp.broadcast_to(row, square), 0.0), axis=1, keepdims=True)
            ready[slot, j] = lagged[j * stations : (j + 1) * stations] * kept
        send(q).start()
        return 0

    turns = count // group
    lax.fori_loop(0, turns, some_rows, 0)
    for q in range(max(turns - 2, 0), turns):
        send(q).wait()


def correlate(part, parts, order, valid, own, chosen, inverse, earlier=None):
    segments, stations, width = own.shape
    steps, block = order.shape
    count = steps * block
    lags = inverse.shape[1]
    group = min(block, 2 * SUB)
    vmem, anywhere = pl.BlockSpec(memory_space=pltpu.VMEM), pl.BlockSpec(memory_space=pl.ANY)
    extra, aliases = ([], {}) if earlier is None else ([earlier], {5: 0})
    return pl.pallas_call(
        functools.partial(correlate_body, part=part, group=group, pair=64 // stations),
        out_shape=jax.ShapeDtypeStruct((steps, block, parts * stations, lags), jnp.float32),
        in_specs=[pl.BlockSpec(memory_space=pltpu.SMEM)] + [vmem] * 4 + [anywhere] * len(extra),
        out_specs=anywhere,
        scratch_shapes=[
            pltpu.VMEM((3, width // 2 // LANES, segments, stations, LANES), jnp.float32),
            pltpu.VMEM((3, width // 2 // LANES, segments * count, LANES), jnp.float32),
            pltpu.VMEM((group * stations, width), jnp.bfloat16),
            pltpu.VMEM((2, group, stations, lags), jnp.float32),
            pltpu.SemaphoreType.DMA((2,)),
        ],
        input_output_aliases=aliases,
        compiler_params=pltpu.CompilerParams(vmem_limit_bytes=16 * 2**20),
        cost_estimate=pl.CostEstimate(
            flops=10**10,
            bytes_accessed=own.size * 2 + chosen.size * 2 + count * stations * lags * 4,
            transcendentals=0,
        ),
    )(order, valid, own, chosen, inverse, *extra)


def swap(block, axis, distance):
    count = lax.axis_size(axis)
    return lax.ppermute(block, axis, [(i, i ^ distance) for i in range(count)])


def local(records, filter_taps, ref_owner, reference_station_order, pair_valid):
    axis = "sta"
    devices = lax.axis_size(axis)
    index = lax.axis_index(axis).astype(jnp.int32)
    stations = records.shape[0] // devices
    width = records.shape[1]

    parts = 2
    wanted, *halves = pick(ref_owner, records.reshape(devices, parts, stations // parts, width))
    pieces = {0: wanted}
    distance = devices
    while distance > 1:
        radix = 4 if distance >= 16 else 2
        distance //= radix
        held = list(pieces.items())
        for j in range(1, radix):
            pieces |= {o | j * distance: swap(p, axis, j * distance) for o, p in held}
    pieces = [pieces[o] for o in range(devices)]

    resident = []
    for p in range(parts):
        resident.append(lax.all_to_all(halves[p], axis, split_axis=0, concat_axis=0))

    band = band_matrix(filter_taps)
    forward = jnp.asarray(forward_matrix(NFFT))
    inverse = jnp.asarray(inverse_transform_matrix(NFFT, LAGS, devices * width // NFFT))
    chosen = whiten(pieces, index[None], band, forward)
    zero = jnp.zeros((1,), jnp.int32)
    result = None
    for p in range(parts):
        own = whiten(resident[p], zero, band, forward)
        result = correlate(p, parts, reference_station_order, pair_valid, own, chosen, inverse, result)
    return result


def solution(mesh):
    placed = (P("win", "sta"), P(), P("win"), P("win", None), P("win", None, "sta"))
    return jax.shard_map(local, mesh=mesh, in_specs=placed, out_specs=P("win", None, "sta", None), check_vma=False)
```

```python
import functools
import math

import jax
import jax.numpy as jnp
import numpy as np
from jax import lax
from jax.experimental import pallas as pl
from jax.experimental.pallas import tpu as pltpu
from jax.sharding import PartitionSpec as P


NFFT = 1024
LAGS = 256
LANES = 128
SUB = 8


def forward_matrix(length):
    time_index = np.arange(length)[:, None]
    bin_index = np.arange(length // 2)[None, :]
    angles = (time_index * bin_index % length).astype(np.float32) * np.float32(2.0 * math.pi / length)
    return np.concatenate([np.cos(angles), -np.sin(angles)], axis=1).astype(jnp.bfloat16)


def inverse_transform_matrix(length, lag_count, segments):
    bin_index = np.arange(length // 2)[:, None]
    shifts = np.arange(lag_count)[None, :] - lag_count // 2
    angles = (bin_index * shifts % length).astype(np.float32) * np.float32(2.0 * math.pi / length)
    factor = np.float32(1.0 / math.sqrt(segments * (length // 2)))
    return np.concatenate([factor * np.cos(angles), -factor * np.sin(angles)], axis=0).astype(jnp.bfloat16)


def pick_body(owner_ref, records_ref, wanted_ref, sems):
    steps, stations, _ = wanted_ref.shape
    copies = []
    for k in range(steps):
        start = pl.multiple_of(owner_ref[k] * stations, stations)
        copies.append(pltpu.make_async_copy(records_ref.at[pl.ds(start, stations)], wanted_ref.at[k], sems.at[k]))
    for copy in copies:
        copy.start()
    for copy in copies:
        copy.wait()


def pick(owner, records, stations):
    steps = owner.shape[0]
    return pl.pallas_call(
        pick_body,
        out_shape=jax.ShapeDtypeStruct((steps, stations, records.shape[1]), records.dtype),
        in_specs=[pl.BlockSpec(memory_space=pltpu.SMEM), pl.BlockSpec(memory_space=pltpu.HBM)],
        out_specs=pl.BlockSpec(memory_space=pltpu.VMEM),
        scratch_shapes=[pltpu.SemaphoreType.DMA((steps,))],
        compiler_params=pltpu.CompilerParams(vmem_limit_bytes=4 * 2**20),
    )(owner, records)


def band_body(row_ref, out_ref):
    width, height = 2 * LANES, 4 * LANES
    rows = jnp.broadcast_to(row_ref[...], (width, height))
    out_ref[...] = pltpu.roll(rows, 0, 1, stride=1, stride_axis=0).T.astype(out_ref.dtype)


def band_matrix(filter_taps):
    count = filter_taps.shape[0]
    before = LANES - (count - 1) // 2
    row = jnp.pad(filter_taps.astype(jnp.float32), (before, 4 * LANES - before - count))[None]
    return pl.pallas_call(
        band_body,
        out_shape=jax.ShapeDtypeStruct((4 * LANES, 2 * LANES), filter_taps.dtype),
        in_specs=[pl.BlockSpec(memory_space=pltpu.VMEM)],
        out_specs=pl.BlockSpec(memory_space=pltpu.VMEM),
        compiler_params=pltpu.CompilerParams(vmem_limit_bytes=4 * 2**20),
    )(row)


def whiten_body(index_ref, *rest, offsets, rows):
    band_ref, forward_ref, out_ref, padded, filtered = rest[-5:]
    stacks = rest[:-5]
    held = [(o, stacks[k].at[i]) for k, some in enumerate(offsets) for i, o in enumerate(some)]
    stations = padded.shape[1]
    width = stacks[0].shape[-1]
    tiles = NFFT // LANES
    parts = width // LANES
    segments = out_ref.shape[0]
    bins = NFFT // 2
    edge = jnp.zeros((stations, LANES), padded.dtype)
    padded[0] = edge
    padded[segments * tiles + 1] = edge
    for offset, piece in held:
        place = 1 + (index_ref[0] ^ offset) * parts
        for part in range(parts):
            padded[place + part] = piece[:, part * LANES : (part + 1) * LANES]
    for first in range(0, segments, rows // stations):
        some = range(first, first + rows // stations)
        for tile in range(0, tiles, 2):
            window = jnp.concatenate(
                [jnp.concatenate([padded[g * tiles + tile + i] for g in some], axis=0) for i in range(4)], axis=1
            )
            filtered[:, tile * LANES : (tile + 2) * LANES] = jnp.dot(
                window, band_ref[...], preferred_element_type=jnp.float32
            ).astype(jnp.bfloat16)
        spectra = jnp.dot(filtered[...], forward_ref[...], preferred_element_type=jnp.float32)
        real_part, imag_part = spectra[:, :bins], spectra[:, bins:]
        energy = real_part * real_part + imag_part * imag_part
        water_level = jnp.sum(energy, axis=-1, keepdims=True) * (1.0 / bins)
        factor = lax.rsqrt(energy + water_level + 1e-06)
        some = slice(first, first + rows // stations)
        out_ref[some, :, :bins] = (real_part * factor).astype(jnp.bfloat16).reshape(-1, stations, bins)
        out_ref[some, :, bins:] = (imag_part * factor).astype(jnp.bfloat16).reshape(-1, stations, bins)


def whiten(raw, offsets, index, band, forward, rows=128):
    _, stations, width = raw[0].shape
    pieces = sum(stack.shape[0] for stack in raw)
    segments = pieces * width // NFFT
    return pl.pallas_call(
        functools.partial(whiten_body, offsets=offsets, rows=rows),
        out_shape=jax.ShapeDtypeStruct((segments, stations, NFFT), jnp.bfloat16),
        in_specs=[pl.BlockSpec(memory_space=pltpu.SMEM)] + [pl.BlockSpec(memory_space=pltpu.VMEM)] * (len(raw) + 2),
        out_specs=pl.BlockSpec(memory_space=pltpu.VMEM),
        scratch_shapes=[
            pltpu.VMEM((segments * NFFT // LANES + 2, stations, LANES), jnp.bfloat16),
            pltpu.VMEM((rows, NFFT), jnp.bfloat16),
        ],
        compiler_params=pltpu.CompilerParams(vmem_limit_bytes=10 * 2**20),
        cost_estimate=pl.CostEstimate(
            flops=2 * segments * stations * NFFT * (NFFT + 512),
            bytes_accessed=2 * segments * stations * NFFT * 2,
            transcendentals=0,
        ),
    )(index, *raw, band, forward)


def correlate_body(step_ref, order_ref, valid_ref, own_ref, chosen_ref, inverse_ref, *rest, group, pair):
    out_ref, own_parts, chosen_parts, cross, ready, sems = rest[-6:]
    segments, stations, width = own_ref.shape
    count = chosen_ref.shape[1]
    step = step_ref[0]
    bins = width // 2
    tiles = bins // LANES

    def prepare(g, _):
        where = pl.ds(pl.multiple_of(g * count, count), count)
        for tile in range(tiles):
            real = slice(tile * LANES, (tile + 1) * LANES)
            imag = slice(bins + tile * LANES, bins + (tile + 1) * LANES)
            c, d = own_ref[g, :, real].astype(jnp.float32), own_ref[g, :, imag].astype(jnp.float32)
            own_parts[0, tile, g], own_parts[1, tile, g], own_parts[2, tile, g] = c, c + d, c - d
            a, b = chosen_ref[g, :, real].astype(jnp.float32), chosen_ref[g, :, imag].astype(jnp.float32)
            chosen_parts[0, tile, where], chosen_parts[1, tile, where], chosen_parts[2, tile, where] = a + b, a, b
        return 0

    lax.fori_loop(0, segments, prepare, 0, unroll=2)
    square = (stations, stations)
    diagonal = lax.broadcasted_iota(jnp.int32, square, 0) == lax.broadcasted_iota(jnp.int32, square, 1)

    def send(q):
        slot = lax.rem(q, 2)
        where = out_ref.at[step, pl.ds(pl.multiple_of(q * group, group), group)]
        return pltpu.make_async_copy(ready.at[slot], where, sems.at[slot])

    def some_rows(q, _):
        start = pl.multiple_of(q * group, group)

        def products(turn, _):
            tile = lax.rem(turn, tiles)
            first = lax.div(turn, tiles) * pair
            picks = [order_ref[step, start + first + j] for j in range(pair)]
            sums = None
            for g in range(segments):
                own = [own_parts[n, tile, g].reshape(stations // SUB, SUB, LANES) for n in range(3)]
                terms = [
                    chosen_parts[n, tile, pl.ds(g * count + pick, SUB, stride=0), :][None] * own[n]
                    for pick in picks
                    for n in range(3)
                ]
                sums = terms if sums is None else [x + y for x, y in zip(sums, terms)]
            for j in range(pair):
                whole, real, imag = [s.reshape(stations, LANES) for s in sums[3 * j : 3 * j + 3]]
                where = pl.ds(pl.multiple_of((first + j) * stations, stations), stations)
                lanes = pl.multiple_of(tile * LANES, LANES)
                cross[where, pl.ds(lanes, LANES)] = (whole - imag).astype(jnp.bfloat16)
                cross[where, pl.ds(bins + lanes, LANES)] = (whole - real).astype(jnp.bfloat16)
            return 0

        lax.fori_loop(0, group // pair * tiles, products, 0)
        lagged = jnp.dot(cross[...], inverse_ref[...], preferred_element_type=jnp.float32)
        valid = valid_ref[step, pl.ds(start, group), :].astype(jnp.float32)

        @pl.when(q >= 2)
        def _():
            send(q - 2).wait()

        slot = lax.rem(q, 2)
        for j in range(group):
            row = valid[j : j + 1]
            kept = jnp.sum(jnp.where(diagonal, jnp.broadcast_to(row, square), 0.0), axis=1, keepdims=True)
            ready[slot, j] = lagged[j * stations : (j + 1) * stations] * kept
        send(q).start()
        return 0

    turns = count // group
    lax.fori_loop(0, turns, some_rows, 0)
    for q in range(max(turns - 2, 0), turns):
        send(q).wait()


def correlate(step, order, valid, own, chosen, inverse, earlier=None):
    segments, stations, width = own.shape
    steps, count = order.shape
    lags = inverse.shape[1]
    group = min(count, SUB)
    vmem, anywhere = pl.BlockSpec(memory_space=pltpu.VMEM), pl.BlockSpec(memory_space=pl.ANY)
    smem = pl.BlockSpec(memory_space=pltpu.SMEM)
    extra, aliases = ([], {}) if earlier is None else ([earlier], {6: 0})
    return pl.pallas_call(
        functools.partial(correlate_body, group=group, pair=2),
        out_shape=jax.ShapeDtypeStruct((steps, count, stations, lags), jnp.float32),
        in_specs=[smem] * 2 + [vmem] * 4 + [anywhere] * len(extra),
        out_specs=anywhere,
        scratch_shapes=[
            pltpu.VMEM((3, width // 2 // LANES, segments, stations, LANES), jnp.float32),
            pltpu.VMEM((3, width // 2 // LANES, segments * count, LANES), jnp.float32),
            pltpu.VMEM((group * stations, width), jnp.bfloat16),
            pltpu.VMEM((2, group, stations, lags), jnp.float32),
            pltpu.SemaphoreType.DMA((2,)),
        ],
        input_output_aliases=aliases,
        compiler_params=pltpu.CompilerParams(vmem_limit_bytes=16 * 2**20),
        cost_estimate=pl.CostEstimate(
            flops=10**10,
            bytes_accessed=own.size * 2 + chosen.size * 2 + count * stations * lags * 4,
            transcendentals=0,
        ),
    )(step, order, valid, own, chosen, inverse, *extra)


def swap(block, axis, distance):
    count = lax.axis_size(axis)
    return lax.ppermute(block, axis, [(i, i ^ distance) for i in range(count)])


def local(records, filter_taps, ref_owner, reference_station_order, pair_valid):
    axis = "sta"
    devices = lax.axis_size(axis)
    index = lax.axis_index(axis).astype(jnp.int32)
    stations = records.shape[0] // devices
    width = records.shape[1]

    wanted = pick(ref_owner, records, stations)
    held, offsets = [wanted[None]], [0]
    distance = devices
    while distance > 2:
        radix = 4 if distance >= 16 else 2
        distance //= radix
        block = jnp.concatenate(held, axis=0)
        held = [block] + [swap(block, axis, j * distance) for j in range(1, radix)]
        offsets = [j * distance | o for j in range(radix) for o in offsets]
    mine = lax.rem(index, 2)
    of_step = lambda k: jnp.concatenate([lax.dynamic_index_in_dim(part, k, 1, keepdims=False) for part in held], axis=0)
    kept = of_step(mine)
    taken = swap(of_step(1 - mine), axis, 1)

    rows = lax.all_to_all(records.reshape(devices, stations, width), axis, split_axis=0, concat_axis=0)

    band = band_matrix(filter_taps)
    forward = jnp.asarray(forward_matrix(NFFT))
    inverse = jnp.asarray(inverse_transform_matrix(NFFT, LAGS, devices * width // NFFT))
    first = whiten([kept, taken], [offsets, [o | 1 for o in offsets]], index[None], band, forward)
    second = swap(first, axis, 1)
    own = whiten([rows], [list(range(devices))], jnp.zeros((1,), jnp.int32), band, forward)
    order = reference_station_order
    done = correlate(mine[None], order, pair_valid, own, first, inverse)
    return correlate(1 - mine[None], order, pair_valid, own, second, inverse, done)


def solution(mesh):
    placed = (P("win", "sta"), P(), P("win"), P("win", None), P("win", None, "sta"))
    return jax.shard_map(local, mesh=mesh, in_specs=placed, out_specs=P("win", None, "sta", None), check_vma=False)
```

```python
import functools
import math

import jax
import jax.numpy as jnp
import numpy as np
from jax import lax
from jax.experimental import pallas as pl
from jax.experimental.pallas import tpu as pltpu
from jax.sharding import PartitionSpec as P


NFFT = 1024
LAGS = 256
LANES = 128
SUB = 8


def forward_matrix(length):
    time_index = np.arange(length)[:, None]
    bin_index = np.arange(length // 2)[None, :]
    angles = (time_index * bin_index % length).astype(np.float32) * np.float32(2.0 * math.pi / length)
    return np.concatenate([np.cos(angles), -np.sin(angles)], axis=1).astype(jnp.bfloat16)


def inverse_transform_matrix(length, lag_count, segments):
    bin_index = np.arange(length // 2)[:, None]
    shifts = np.arange(lag_count)[None, :] - lag_count // 2
    angles = (bin_index * shifts % length).astype(np.float32) * np.float32(2.0 * math.pi / length)
    factor = np.float32(1.0 / math.sqrt(segments * (length // 2)))
    return np.concatenate([factor * np.cos(angles), -factor * np.sin(angles)], axis=0).astype(jnp.bfloat16)


def pick_body(owner_ref, records_ref, wanted_ref, sems):
    steps, stations, _ = wanted_ref.shape
    copies = []
    for k in range(steps):
        start = pl.multiple_of(owner_ref[k] * stations, stations)
        copies.append(pltpu.make_async_copy(records_ref.at[pl.ds(start, stations)], wanted_ref.at[k], sems.at[k]))
    for copy in copies:
        copy.start()
    for copy in copies:
        copy.wait()


def pick(owner, records, stations):
    steps = owner.shape[0]
    return pl.pallas_call(
        pick_body,
        out_shape=jax.ShapeDtypeStruct((steps, stations, records.shape[1]), records.dtype),
        in_specs=[pl.BlockSpec(memory_space=pltpu.SMEM), pl.BlockSpec(memory_space=pltpu.HBM)],
        out_specs=pl.BlockSpec(memory_space=pltpu.VMEM),
        scratch_shapes=[pltpu.SemaphoreType.DMA((steps,))],
        compiler_params=pltpu.CompilerParams(vmem_limit_bytes=60 * 2**20),
    )(owner, records)


def band_body(row_ref, out_ref):
    width, height = 2 * LANES, 4 * LANES
    rows = jnp.broadcast_to(row_ref[...], (width, height))
    out_ref[...] = pltpu.roll(rows, 0, 1, stride=1, stride_axis=0).T.astype(out_ref.dtype)


def band_matrix(filter_taps):
    count = filter_taps.shape[0]
    before = LANES - (count - 1) // 2
    row = jnp.pad(filter_taps.astype(jnp.float32), (before, 4 * LANES - before - count))[None]
    return pl.pallas_call(
        band_body,
        out_shape=jax.ShapeDtypeStruct((4 * LANES, 2 * LANES), filter_taps.dtype),
        in_specs=[pl.BlockSpec(memory_space=pltpu.VMEM)],
        out_specs=pl.BlockSpec(memory_space=pltpu.VMEM),
        compiler_params=pltpu.CompilerParams(vmem_limit_bytes=4 * 2**20),
    )(row)


def whiten_body(index_ref, *rest, offsets, rows):
    band_ref, forward_source, out_ref, padded, filtered, forward_ref, sem = rest[-7:]
    brought = pltpu.make_async_copy(forward_source, forward_ref, sem)
    brought.start()
    stacks = rest[:-7]
    held = [(o, stacks[k].at[i]) for k, some in enumerate(offsets) for i, o in enumerate(some)]
    stations = padded.shape[1]
    width = stacks[0].shape[-1]
    tiles = NFFT // LANES
    parts = width // LANES
    segments = out_ref.shape[0]
    bins = NFFT // 2
    edge = jnp.zeros((stations, LANES), padded.dtype)
    padded[0] = edge
    padded[segments * tiles + 1] = edge
    for offset, piece in held:
        place = 1 + (index_ref[0] ^ offset) * parts
        for part in range(parts):
            padded[place + part] = piece[:, part * LANES : (part + 1) * LANES]
    for first in range(0, segments, rows // stations):
        some = range(first, first + rows // stations)
        for tile in range(0, tiles, 2):
            window = jnp.concatenate(
                [jnp.concatenate([padded[g * tiles + tile + i] for g in some], axis=0) for i in range(4)], axis=1
            )
            filtered[first * stations : first * stations + rows, tile * LANES : (tile + 2) * LANES] = jnp.dot(
                window, band_ref[...], preferred_element_type=jnp.float32
            ).astype(jnp.bfloat16)
    brought.wait()
    for first in range(0, segments, rows // stations):
        spectra = jnp.dot(
            filtered[first * stations : first * stations + rows], forward_ref[...], preferred_element_type=jnp.float32
        )
        real_part, imag_part = spectra[:, :bins], spectra[:, bins:]
        energy = real_part * real_part + imag_part * imag_part
        water_level = jnp.sum(energy, axis=-1, keepdims=True) * (1.0 / bins)
        factor = lax.rsqrt(energy + water_level + 1e-06)
        some = slice(first, first + rows // stations)
        out_ref[some, :, :bins] = (real_part * factor).astype(jnp.bfloat16).reshape(-1, stations, bins)
        out_ref[some, :, bins:] = (imag_part * factor).astype(jnp.bfloat16).reshape(-1, stations, bins)


def whiten(raw, offsets, index, band, forward, rows=128):
    _, stations, width = raw[0].shape
    pieces = sum(stack.shape[0] for stack in raw)
    segments = pieces * width // NFFT
    return pl.pallas_call(
        functools.partial(whiten_body, offsets=offsets, rows=rows),
        out_shape=jax.ShapeDtypeStruct((segments, stations, NFFT), jnp.bfloat16),
        in_specs=[pl.BlockSpec(memory_space=pltpu.SMEM)] + [pl.BlockSpec(memory_space=pltpu.VMEM)] * (len(raw) + 1)
        + [pl.BlockSpec(memory_space=pl.ANY)],
        out_specs=pl.BlockSpec(memory_space=pltpu.VMEM),
        scratch_shapes=[
            pltpu.VMEM((segments * NFFT // LANES + 2, stations, LANES), jnp.bfloat16),
            pltpu.VMEM((segments * stations, NFFT), jnp.bfloat16),
            pltpu.VMEM(forward.shape, forward.dtype),
            pltpu.SemaphoreType.DMA,
        ],
        compiler_params=pltpu.CompilerParams(vmem_limit_bytes=50 * 2**20),
        cost_estimate=pl.CostEstimate(
            flops=2 * segments * stations * NFFT * (NFFT + 512),
            bytes_accessed=2 * segments * stations * NFFT * 2,
            transcendentals=0,
        ),
    )(index, *raw, band, forward)


def correlate_body(
    mine_ref, order_ref, valid_ref, own_ref, first_ref, second_ref, inverse_ref, out_ref, *rest, group, unroll, pitch
):
    paired, products, cross, ready, sems = rest
    segments, stations, width = own_ref.shape
    steps, block = order_ref.shape
    count = steps * block
    bins = width // 2
    tiles = bins // LANES
    depth = 2 * segments
    half = 2 * stations
    (near, far), (near_out, far_out) = pitch
    mine = mine_ref[0]

    def arrange(g, _):
        for tile in range(tiles):
            real = slice(tile * LANES, (tile + 1) * LANES)
            imag = slice(bins + tile * LANES, bins + (tile + 1) * LANES)
            re, im = own_ref[g, :, real], own_ref[g, :, imag]
            for part in range(2):
                lanes = imag if part else real
                chosen = [first_ref[g, :, lanes], second_ref[g, :, lanes]]
                resident = [im, re] if part else [re, -im]
                stack = jnp.concatenate(resident + chosen if tile % 2 == 0 else chosen + resident, axis=0)
                where = pl.ds((part * segments + g) * near + tile, LANES, stride=far)
                paired[where, :] = stack.T.astype(jnp.float32)
        return 0

    lax.fori_loop(0, segments, arrange, 0)
    low = lax.broadcasted_iota(jnp.int32, (depth, LANES), 1) < half
    column = lax.broadcasted_iota(jnp.int32, (count, tiles * depth), 1)
    even = lax.rem(lax.div(column, depth), 2) == 0
    none = jnp.zeros((), jnp.bfloat16)
    zeros = jnp.zeros((depth, LANES), jnp.bfloat16)

    def multiply(q, _):
        parts = [
            paired[pl.ds(q * far + tile, depth, stride=near), :].astype(jnp.bfloat16) for tile in range(tiles)
        ]
        turned = jnp.concatenate(parts, axis=0).T
        left = jnp.where(even, turned[half:], turned[:half])
        right = []
        for tile in range(tiles):
            kept = jnp.where(low if tile % 2 == 0 else ~low, parts[tile], none)
            blocks = [zeros] * (tiles // 2)
            blocks[tile // 2] = kept
            right.append(jnp.concatenate(blocks, axis=1))
        result = jnp.dot(left, jnp.concatenate(right, axis=0), preferred_element_type=jnp.float32)
        for h in range(tiles // 2):
            products[pl.ds(q * far_out + h, count, stride=near_out), :] = result[:, h * LANES : (h + 1) * LANES]
        return 0

    lax.fori_loop(0, LANES, multiply, 0, unroll=unroll)
    square = (stations, stations)
    diagonal = lax.broadcasted_iota(jnp.int32, square, 0) == lax.broadcasted_iota(jnp.int32, square, 1)
    turns = count // group

    def place(n):
        return lax.div(n, block // group), pl.multiple_of(lax.rem(n, block // group) * group, group)

    def send(n):
        step, start = place(n)
        slot = lax.rem(n, 2)
        return pltpu.make_async_copy(ready.at[slot], out_ref.at[step, pl.ds(start, group)], sems.at[slot])

    def finish(n, _):
        step, start = place(n)
        for j in range(group):
            row = (step ^ mine) * block + order_ref[step, start + j]
            for h in range(tiles // 2):
                turned = products[pl.ds(row * near_out + h, LANES, stride=far_out), :].astype(jnp.bfloat16).T
                for tile in range(2):
                    for part in range(2):
                        at = (2 * tile + part) * stations
                        lane = part * bins + (2 * h + tile) * LANES
                        cross[j * stations : (j + 1) * stations, lane : lane + LANES] = turned[at : at + stations]
        lagged = jnp.dot(cross[...], inverse_ref[...], preferred_element_type=jnp.float32)
        valid = valid_ref[step, pl.ds(start, group), :].astype(jnp.float32)

        @pl.when(n >= 2)
        def _():
            send(n - 2).wait()

        slot = lax.rem(n, 2)
        for j in range(group):
            kept = jnp.sum(
                jnp.where(diagonal, jnp.broadcast_to(valid[j : j + 1], square), 0.0), axis=1, keepdims=True
            )
            ready[slot, j] = lagged[j * stations : (j + 1) * stations] * kept
        send(n).start()
        return 0

    lax.fori_loop(0, turns, finish, 0)
    for n in range(max(turns - 2, 0), turns):
        send(n).wait()


def correlate(mine, order, valid, own, first, second, inverse):
    segments, stations, width = own.shape
    steps, block = order.shape
    count = steps * block
    lags = inverse.shape[1]
    tiles = width // 2 // LANES
    depth = 2 * segments
    assert steps == 2 and tiles * depth == LANES and 2 * stations == count and 4 * stations == LANES
    group = min(block, 2 * SUB)
    near, near_out = tiles + 1, tiles // 2 + 1
    pitch = (near, near * depth + 1), (near_out, near_out * count + 1)
    vmem, smem = pl.BlockSpec(memory_space=pltpu.VMEM), pl.BlockSpec(memory_space=pltpu.SMEM)
    return pl.pallas_call(
        functools.partial(correlate_body, group=group, unroll=16, pitch=pitch),
        out_shape=jax.ShapeDtypeStruct((steps, block, stations, lags), jnp.float32),
        in_specs=[smem] * 2 + [vmem] * 5,
        out_specs=pl.BlockSpec(memory_space=pl.ANY),
        scratch_shapes=[
            pltpu.VMEM((LANES * pitch[0][1], LANES), jnp.float32),
            pltpu.VMEM((LANES * pitch[1][1], LANES), jnp.float32),
            pltpu.VMEM((group * stations, width), jnp.bfloat16),
            pltpu.VMEM((2, group, stations, lags), jnp.float32),
            pltpu.SemaphoreType.DMA((2,)),
        ],
        compiler_params=pltpu.CompilerParams(vmem_limit_bytes=30 * 2**20),
        cost_estimate=pl.CostEstimate(
            flops=10**10,
            bytes_accessed=(own.size + first.size + second.size) * 2 + count * stations * lags * 4,
            transcendentals=0,
        ),
    )(mine, order, valid, own, first, second, inverse)


def swap(block, axis, distance):
    count = lax.axis_size(axis)
    return lax.ppermute(block, axis, [(i, i ^ distance) for i in range(count)])


def local(records, filter_taps, ref_owner, reference_station_order, pair_valid):
    axis = "sta"
    devices = lax.axis_size(axis)
    index = lax.axis_index(axis).astype(jnp.int32)
    stations = records.shape[0] // devices
    width = records.shape[1]

    wanted = pick(ref_owner, records, stations)
    held, offsets = [wanted[None]], [0]
    distance = devices
    while distance > 2:
        radix = 4 if distance >= 16 else 2
        distance //= radix
        block = jnp.concatenate(held, axis=0)
        held = [block] + [swap(block, axis, j * distance) for j in range(1, radix)]
        offsets = [j * distance | o for j in range(radix) for o in offsets]
    mine = lax.rem(index, 2)
    of_step = lambda k: jnp.concatenate([lax.dynamic_index_in_dim(part, k, 1, keepdims=False) for part in held], axis=0)
    kept = of_step(mine)
    taken = swap(of_step(1 - mine), axis, 1)

    rows = lax.all_to_all(records.reshape(devices, stations, width), axis, split_axis=0, concat_axis=0)

    band = band_matrix(filter_taps)
    forward = jnp.asarray(forward_matrix(NFFT))
    inverse = jnp.asarray(inverse_transform_matrix(NFFT, LAGS, devices * width // NFFT))
    first = whiten([kept, taken], [offsets, [o | 1 for o in offsets]], index[None], band, forward)
    second = swap(first, axis, 1)
    own = whiten([rows], [list(range(devices))], jnp.zeros((1,), jnp.int32), band, forward)
    return correlate(mine[None], reference_station_order, pair_valid, own, first, second, inverse)


def solution(mesh):
    placed = (P("win", "sta"), P(), P("win"), P("win", None), P("win", None, "sta"))
    return jax.shard_map(local, mesh=mesh, in_specs=placed, out_specs=P("win", None, "sta", None), check_vma=False)
```

```python
import functools
import math

import jax
import jax.numpy as jnp
import numpy as np
from jax import lax
from jax.experimental import pallas as pl
from jax.experimental.pallas import tpu as pltpu
from jax.sharding import PartitionSpec as P


NFFT = 1024
LAGS = 256
LANES = 128
SUB = 8


def forward_matrix(length):
    time_index = np.arange(length)[:, None]
    bin_index = np.arange(length // 2)[None, :]
    angles = (time_index * bin_index % length).astype(np.float32) * np.float32(2.0 * math.pi / length)
    return np.concatenate([np.cos(angles), -np.sin(angles)], axis=1).astype(jnp.bfloat16)


def inverse_transform_matrix(length, lag_count, segments):
    bin_index = np.arange(length // 2)[:, None]
    shifts = np.arange(lag_count)[None, :] - lag_count // 2
    angles = (bin_index * shifts % length).astype(np.float32) * np.float32(2.0 * math.pi / length)
    factor = np.float32(1.0 / math.sqrt(segments * (length // 2)))
    return np.concatenate([factor * np.cos(angles), -factor * np.sin(angles)], axis=0).astype(jnp.bfloat16)


def pick_body(owner_ref, records_ref, wanted_ref, sems):
    steps, stations, _ = wanted_ref.shape
    copies = []
    for k in range(steps):
        start = pl.multiple_of(owner_ref[k] * stations, stations)
        copies.append(pltpu.make_async_copy(records_ref.at[pl.ds(start, stations)], wanted_ref.at[k], sems.at[k]))
    for copy in copies:
        copy.start()
    for copy in copies:
        copy.wait()


def pick(owner, records, stations):
    steps = owner.shape[0]
    return pl.pallas_call(
        pick_body,
        out_shape=jax.ShapeDtypeStruct((steps, stations, records.shape[1]), records.dtype),
        in_specs=[pl.BlockSpec(memory_space=pltpu.SMEM), pl.BlockSpec(memory_space=pltpu.HBM)],
        out_specs=pl.BlockSpec(memory_space=pltpu.VMEM),
        scratch_shapes=[pltpu.SemaphoreType.DMA((steps,))],
        compiler_params=pltpu.CompilerParams(vmem_limit_bytes=60 * 2**20),
    )(owner, records)


def band_body(row_ref, out_ref):
    width, height = 2 * LANES, 4 * LANES
    rows = jnp.broadcast_to(row_ref[...], (width, height))
    out_ref[...] = pltpu.roll(rows, 0, 1, stride=1, stride_axis=0).T.astype(out_ref.dtype)


def band_matrix(filter_taps):
    count = filter_taps.shape[0]
    before = LANES - (count - 1) // 2
    row = jnp.pad(filter_taps.astype(jnp.float32), (before, 4 * LANES - before - count))[None]
    return pl.pallas_call(
        band_body,
        out_shape=jax.ShapeDtypeStruct((4 * LANES, 2 * LANES), filter_taps.dtype),
        in_specs=[pl.BlockSpec(memory_space=pltpu.VMEM)],
        out_specs=pl.BlockSpec(memory_space=pltpu.VMEM),
        compiler_params=pltpu.CompilerParams(vmem_limit_bytes=4 * 2**20),
    )(row)


def fetch_body(source_ref, out_ref, sem):
    copy = pltpu.make_async_copy(source_ref, out_ref, sem)
    copy.start()
    copy.wait()


def fetch(matrix):
    return pl.pallas_call(
        fetch_body,
        out_shape=jax.ShapeDtypeStruct(matrix.shape, matrix.dtype),
        in_specs=[pl.BlockSpec(memory_space=pltpu.HBM)],
        out_specs=pl.BlockSpec(memory_space=pltpu.VMEM),
        scratch_shapes=[pltpu.SemaphoreType.DMA],
        compiler_params=pltpu.CompilerParams(vmem_limit_bytes=50 * 2**20),
    )(matrix)


def whiten_body(index_ref, *rest, offsets, rows):
    band_ref, forward_ref, out_ref, padded, filtered = rest[-5:]
    stacks = rest[:-5]
    held = [(o, stacks[k].at[i]) for k, some in enumerate(offsets) for i, o in enumerate(some)]
    stations = padded.shape[1]
    width = stacks[0].shape[-1]
    tiles = NFFT // LANES
    parts = width // LANES
    segments = out_ref.shape[0]
    bins = NFFT // 2
    edge = jnp.zeros((stations, LANES), padded.dtype)
    padded[0] = edge
    padded[segments * tiles + 1] = edge
    for offset, piece in held:
        place = 1 + (index_ref[0] ^ offset) * parts
        for part in range(parts):
            padded[place + part] = piece[:, part * LANES : (part + 1) * LANES]
    for first in range(0, segments, rows // stations):
        some = range(first, first + rows // stations)
        for tile in range(0, tiles, 2):
            window = jnp.concatenate(
                [jnp.concatenate([padded[g * tiles + tile + i] for g in some], axis=0) for i in range(4)], axis=1
            )
            filtered[:, tile * LANES : (tile + 2) * LANES] = jnp.dot(
                window, band_ref[...], preferred_element_type=jnp.float32
            ).astype(jnp.bfloat16)
        spectra = jnp.dot(filtered[...], forward_ref[...], preferred_element_type=jnp.float32)
        real_part, imag_part = spectra[:, :bins], spectra[:, bins:]
        energy = real_part * real_part + imag_part * imag_part
        water_level = jnp.sum(energy, axis=-1, keepdims=True) * (1.0 / bins)
        factor = lax.rsqrt(energy + water_level + 1e-06)
        some = slice(first, first + rows // stations)
        out_ref[some, :, :bins] = (real_part * factor).astype(jnp.bfloat16).reshape(-1, stations, bins)
        out_ref[some, :, bins:] = (imag_part * factor).astype(jnp.bfloat16).reshape(-1, stations, bins)


def whiten(raw, offsets, index, band, forward, rows=128):
    _, stations, width = raw[0].shape
    pieces = sum(stack.shape[0] for stack in raw)
    segments = pieces * width // NFFT
    return pl.pallas_call(
        functools.partial(whiten_body, offsets=offsets, rows=rows),
        out_shape=jax.ShapeDtypeStruct((segments, stations, NFFT), jnp.bfloat16),
        in_specs=[pl.BlockSpec(memory_space=pltpu.SMEM)] + [pl.BlockSpec(memory_space=pltpu.VMEM)] * (len(raw) + 2),
        out_specs=pl.BlockSpec(memory_space=pltpu.VMEM),
        scratch_shapes=[
            pltpu.VMEM((segments * NFFT // LANES + 2, stations, LANES), jnp.bfloat16),
            pltpu.VMEM((rows, NFFT), jnp.bfloat16),
        ],
        compiler_params=pltpu.CompilerParams(vmem_limit_bytes=10 * 2**20),
        cost_estimate=pl.CostEstimate(
            flops=2 * segments * stations * NFFT * (NFFT + 512),
            bytes_accessed=2 * segments * stations * NFFT * 2,
            transcendentals=0,
        ),
    )(index, *raw, band, forward)


def correlate_body(
    mine_ref, order_ref, valid_ref, own_ref, first_ref, second_ref, inverse_ref, out_ref, *rest, group, unroll, pitch
):
    paired, products, cross, ready, sems = rest
    segments, stations, width = own_ref.shape
    steps, block = order_ref.shape
    count = steps * block
    bins = width // 2
    tiles = bins // LANES
    depth = 2 * segments
    half = 2 * stations
    (near, far), (near_out, far_out) = pitch
    mine = mine_ref[0]

    def arrange(g, _):
        for tile in range(tiles):
            real = slice(tile * LANES, (tile + 1) * LANES)
            imag = slice(bins + tile * LANES, bins + (tile + 1) * LANES)
            re, im = own_ref[g, :, real], own_ref[g, :, imag]
            for part in range(2):
                lanes = imag if part else real
                chosen = [first_ref[g, :, lanes], second_ref[g, :, lanes]]
                resident = [im, re] if part else [re, -im]
                stack = jnp.concatenate(resident + chosen if tile % 2 == 0 else chosen + resident, axis=0)
                where = pl.ds((part * segments + g) * near + tile, LANES, stride=far)
                paired[where, :] = stack.T.astype(jnp.float32)
        return 0

    lax.fori_loop(0, segments, arrange, 0)
    low = lax.broadcasted_iota(jnp.int32, (depth, LANES), 1) < half
    column = lax.broadcasted_iota(jnp.int32, (count, tiles * depth), 1)
    even = lax.rem(lax.div(column, depth), 2) == 0
    none = jnp.zeros((), jnp.bfloat16)
    zeros = jnp.zeros((depth, LANES), jnp.bfloat16)

    def multiply(q, _):
        parts = [
            paired[pl.ds(q * far + tile, depth, stride=near), :].astype(jnp.bfloat16) for tile in range(tiles)
        ]
        turned = jnp.concatenate(parts, axis=0).T
        left = jnp.where(even, turned[half:], turned[:half])
        right = []
        for tile in range(tiles):
            kept = jnp.where(low if tile % 2 == 0 else ~low, parts[tile], none)
            blocks = [zeros] * (tiles // 2)
            blocks[tile // 2] = kept
            right.append(jnp.concatenate(blocks, axis=1))
        result = jnp.dot(left, jnp.concatenate(right, axis=0), preferred_element_type=jnp.float32)
        for h in range(tiles // 2):
            products[pl.ds(q * far_out + h, count, stride=near_out), :] = result[:, h * LANES : (h + 1) * LANES]
        return 0

    lax.fori_loop(0, LANES, multiply, 0, unroll=unroll)
    square = (stations, stations)
    diagonal = lax.broadcasted_iota(jnp.int32, square, 0) == lax.broadcasted_iota(jnp.int32, square, 1)
    turns = count // group

    def place(n):
        return lax.div(n, block // group), pl.multiple_of(lax.rem(n, block // group) * group, group)

    def send(n):
        step, start = place(n)
        slot = lax.rem(n, 2)
        return pltpu.make_async_copy(ready.at[slot], out_ref.at[step, pl.ds(start, group)], sems.at[slot])

    def finish(n, _):
        step, start = place(n)
        for j in range(group):
            row = (step ^ mine) * block + order_ref[step, start + j]
            for h in range(tiles // 2):
                turned = products[pl.ds(row * near_out + h, LANES, stride=far_out), :].astype(jnp.bfloat16).T
                for tile in range(2):
                    for part in range(2):
                        at = (2 * tile + part) * stations
                        lane = part * bins + (2 * h + tile) * LANES
                        cross[j * stations : (j + 1) * stations, lane : lane + LANES] = turned[at : at + stations]
        lagged = jnp.dot(cross[...], inverse_ref[...], preferred_element_type=jnp.float32)
        valid = valid_ref[step, pl.ds(start, group), :].astype(jnp.float32)

        @pl.when(n >= 2)
        def _():
            send(n - 2).wait()

        slot = lax.rem(n, 2)
        for j in range(group):
            kept = jnp.sum(
                jnp.where(diagonal, jnp.broadcast_to(valid[j : j + 1], square), 0.0), axis=1, keepdims=True
            )
            ready[slot, j] = lagged[j * stations : (j + 1) * stations] * kept
        send(n).start()
        return 0

    lax.fori_loop(0, turns, finish, 0)
    for n in range(max(turns - 2, 0), turns):
        send(n).wait()


def correlate(mine, order, valid, own, first, second, inverse):
    segments, stations, width = own.shape
    steps, block = order.shape
    count = steps * block
    lags = inverse.shape[1]
    tiles = width // 2 // LANES
    depth = 2 * segments
    assert steps == 2 and tiles * depth == LANES and 2 * stations == count and 4 * stations == LANES
    group = min(block, 2 * SUB)
    near, near_out = tiles + 1, tiles // 2 + 1
    pitch = (near, near * depth + 1), (near_out, near_out * count + 1)
    vmem, smem = pl.BlockSpec(memory_space=pltpu.VMEM), pl.BlockSpec(memory_space=pltpu.SMEM)
    return pl.pallas_call(
        functools.partial(correlate_body, group=group, unroll=16, pitch=pitch),
        out_shape=jax.ShapeDtypeStruct((steps, block, stations, lags), jnp.float32),
        in_specs=[smem] * 2 + [vmem] * 5,
        out_specs=pl.BlockSpec(memory_space=pl.ANY),
        scratch_shapes=[
            pltpu.VMEM((LANES * pitch[0][1], LANES), jnp.float32),
            pltpu.VMEM((LANES * pitch[1][1], LANES), jnp.float32),
            pltpu.VMEM((group * stations, width), jnp.bfloat16),
            pltpu.VMEM((2, group, stations, lags), jnp.float32),
            pltpu.SemaphoreType.DMA((2,)),
        ],
        compiler_params=pltpu.CompilerParams(vmem_limit_bytes=30 * 2**20),
        cost_estimate=pl.CostEstimate(
            flops=10**10,
            bytes_accessed=(own.size + first.size + second.size) * 2 + count * stations * lags * 4,
            transcendentals=0,
        ),
    )(mine, order, valid, own, first, second, inverse)


def swap(block, axis, distance):
    count = lax.axis_size(axis)
    return lax.ppermute(block, axis, [(i, i ^ distance) for i in range(count)])


def local(records, filter_taps, ref_owner, reference_station_order, pair_valid):
    axis = "sta"
    devices = lax.axis_size(axis)
    index = lax.axis_index(axis).astype(jnp.int32)
    stations = records.shape[0] // devices
    width = records.shape[1]

    wanted = pick(ref_owner, records, stations)
    held, offsets = [wanted[None]], [0]
    distance = devices
    while distance > 2:
        radix = 4 if distance >= 16 else 2
        distance //= radix
        block = jnp.concatenate(held, axis=0)
        held = [block] + [swap(block, axis, j * distance) for j in range(1, radix)]
        offsets = [j * distance | o for j in range(radix) for o in offsets]
    mine = lax.rem(index, 2)
    of_step = lambda k: jnp.concatenate([lax.dynamic_index_in_dim(part, k, 1, keepdims=False) for part in held], axis=0)
    kept = of_step(mine)
    taken = swap(of_step(1 - mine), axis, 1)

    rows = lax.all_to_all(records.reshape(devices, stations, width), axis, split_axis=0, concat_axis=0)

    band = band_matrix(filter_taps)
    forward = fetch(jnp.asarray(forward_matrix(NFFT)))
    inverse = jnp.asarray(inverse_transform_matrix(NFFT, LAGS, devices * width // NFFT))
    first = whiten([kept, taken], [offsets, [o | 1 for o in offsets]], index[None], band, forward)
    second = swap(first, axis, 1)
    own = whiten([rows], [list(range(devices))], jnp.zeros((1,), jnp.int32), band, forward)
    return correlate(mine[None], reference_station_order, pair_valid, own, first, second, inverse)


def solution(mesh):
    placed = (P("win", "sta"), P(), P("win"), P("win", None), P("win", None, "sta"))
    return jax.shard_map(local, mesh=mesh, in_specs=placed, out_specs=P("win", None, "sta", None), check_vma=False)
```

```python
import functools
import math

import jax
import jax.numpy as jnp
import numpy as np
from jax import lax
from jax.experimental import pallas as pl
from jax.experimental.pallas import tpu as pltpu
from jax.sharding import PartitionSpec as P


NFFT = 1024
LAGS = 256
LANES = 128


def forward_matrix(length):
    time_index = np.arange(length)[:, None]
    bin_index = np.arange(length // 2)[None, :]
    angles = (time_index * bin_index % length).astype(np.float32) * np.float32(2.0 * math.pi / length)
    return np.concatenate([np.cos(angles), -np.sin(angles)], axis=1).astype(jnp.bfloat16)


def inverse_transform_matrix(length, lag_count, segments):
    bin_index = np.arange(length // 2)[:, None]
    shifts = np.arange(lag_count)[None, :] - lag_count // 2
    angles = (bin_index * shifts % length).astype(np.float32) * np.float32(2.0 * math.pi / length)
    factor = np.float32(1.0 / math.sqrt(segments * (length // 2)))
    return np.concatenate([factor * np.cos(angles), -factor * np.sin(angles)], axis=0).astype(jnp.bfloat16)


def pick_body(owner_ref, records_ref, wanted_ref, sems):
    steps, stations, _ = wanted_ref.shape
    copies = []
    for k in range(steps):
        start = pl.multiple_of(owner_ref[k] * stations, stations)
        copies.append(pltpu.make_async_copy(records_ref.at[pl.ds(start, stations)], wanted_ref.at[k], sems.at[k]))
    for copy in copies:
        copy.start()
    for copy in copies:
        copy.wait()


def pick(owner, records, stations):
    steps = owner.shape[0]
    return pl.pallas_call(
        pick_body,
        out_shape=jax.ShapeDtypeStruct((steps, stations, records.shape[1]), records.dtype),
        in_specs=[pl.BlockSpec(memory_space=pltpu.SMEM), pl.BlockSpec(memory_space=pltpu.HBM)],
        out_specs=pl.BlockSpec(memory_space=pltpu.VMEM),
        scratch_shapes=[pltpu.SemaphoreType.DMA((steps,))],
        compiler_params=pltpu.CompilerParams(vmem_limit_bytes=60 * 2**20),
    )(owner, records)


def band_body(row_ref, out_ref):
    width, height = 2 * LANES, 4 * LANES
    rows = jnp.broadcast_to(row_ref[...], (width, height))
    out_ref[...] = pltpu.roll(rows, 0, 1, stride=1, stride_axis=0).T.astype(out_ref.dtype)


def band_matrix(filter_taps):
    count = filter_taps.shape[0]
    before = LANES - (count - 1) // 2
    row = jnp.pad(filter_taps.astype(jnp.float32), (before, 4 * LANES - before - count))[None]
    return pl.pallas_call(
        band_body,
        out_shape=jax.ShapeDtypeStruct((4 * LANES, 2 * LANES), filter_taps.dtype),
        in_specs=[pl.BlockSpec(memory_space=pltpu.VMEM)],
        out_specs=pl.BlockSpec(memory_space=pltpu.VMEM),
        compiler_params=pltpu.CompilerParams(vmem_limit_bytes=4 * 2**20),
    )(row)


def fetch_body(source_ref, out_ref, sem):
    copy = pltpu.make_async_copy(source_ref, out_ref, sem)
    copy.start()
    copy.wait()


def fetch(matrix):
    return pl.pallas_call(
        fetch_body,
        out_shape=jax.ShapeDtypeStruct(matrix.shape, matrix.dtype),
        in_specs=[pl.BlockSpec(memory_space=pltpu.HBM)],
        out_specs=pl.BlockSpec(memory_space=pltpu.VMEM),
        scratch_shapes=[pltpu.SemaphoreType.DMA],
        compiler_params=pltpu.CompilerParams(vmem_limit_bytes=50 * 2**20),
    )(matrix)


def whiten_body(index_ref, *rest, offsets, rows):
    band_ref, forward_ref, out_ref, padded, filtered = rest[-5:]
    stacks = rest[:-5]
    held = [(o, stacks[k].at[i]) for k, some in enumerate(offsets) for i, o in enumerate(some)]
    stations = padded.shape[1]
    width = stacks[0].shape[-1]
    tiles = NFFT // LANES
    parts = width // LANES
    segments = out_ref.shape[0]
    bins = NFFT // 2
    edge = jnp.zeros((stations, LANES), padded.dtype)
    padded[0] = edge
    padded[segments * tiles + 1] = edge
    for offset, piece in held:
        place = 1 + (index_ref[0] ^ offset) * parts
        for part in range(parts):
            padded[place + part] = piece[:, part * LANES : (part + 1) * LANES]
    for first in range(0, segments, rows // stations):
        some = range(first, first + rows // stations)
        for tile in range(0, tiles, 2):
            window = jnp.concatenate(
                [jnp.concatenate([padded[g * tiles + tile + i] for g in some], axis=0) for i in range(4)], axis=1
            )
            filtered[:, tile * LANES : (tile + 2) * LANES] = jnp.dot(
                window, band_ref[...], preferred_element_type=jnp.float32
            ).astype(jnp.bfloat16)
        spectra = jnp.dot(filtered[...], forward_ref[...], preferred_element_type=jnp.float32)
        real_part, imag_part = spectra[:, :bins], spectra[:, bins:]
        energy = real_part * real_part + imag_part * imag_part
        water_level = jnp.sum(energy, axis=-1, keepdims=True) * (1.0 / bins)
        factor = lax.rsqrt(energy + water_level + 1e-06)
        some = slice(first, first + rows // stations)
        out_ref[some, :, :bins] = (real_part * factor).astype(jnp.bfloat16).reshape(-1, stations, bins)
        out_ref[some, :, bins:] = (imag_part * factor).astype(jnp.bfloat16).reshape(-1, stations, bins)


def whiten(raw, offsets, index, band, forward, rows=128):
    _, stations, width = raw[0].shape
    pieces = sum(stack.shape[0] for stack in raw)
    segments = pieces * width // NFFT
    return pl.pallas_call(
        functools.partial(whiten_body, offsets=offsets, rows=rows),
        out_shape=jax.ShapeDtypeStruct((segments, stations, NFFT), jnp.bfloat16),
        in_specs=[pl.BlockSpec(memory_space=pltpu.SMEM)] + [pl.BlockSpec(memory_space=pltpu.VMEM)] * (len(raw) + 2),
        out_specs=pl.BlockSpec(memory_space=pltpu.VMEM),
        scratch_shapes=[
            pltpu.VMEM((segments * NFFT // LANES + 2, stations, LANES), jnp.bfloat16),
            pltpu.VMEM((rows, NFFT), jnp.bfloat16),
        ],
        compiler_params=pltpu.CompilerParams(vmem_limit_bytes=10 * 2**20),
        cost_estimate=pl.CostEstimate(
            flops=2 * segments * stations * NFFT * (NFFT + 512),
            bytes_accessed=2 * segments * stations * NFFT * 2,
            transcendentals=0,
        ),
    )(index, *raw, band, forward)


def correlate_body(
    mine_ref, order_ref, valid_ref, own_ref, first_ref, second_ref, inverse_ref, out_ref, *rest, group, unroll, pitch
):
    paired, products, cross, ready, sems = rest
    segments, stations, width = own_ref.shape
    steps, block = order_ref.shape
    count = steps * block
    bins = width // 2
    tiles = bins // LANES
    depth = 2 * segments
    half = 2 * stations
    (near, far), (near_out, far_out) = pitch
    mine = mine_ref[0]

    def arrange(g, _):
        for tile in range(tiles):
            real = slice(tile * LANES, (tile + 1) * LANES)
            imag = slice(bins + tile * LANES, bins + (tile + 1) * LANES)
            re, im = own_ref[g, :, real], own_ref[g, :, imag]
            for part in range(2):
                lanes = imag if part else real
                chosen = [first_ref[g, :, lanes], second_ref[g, :, lanes]]
                resident = [im, re] if part else [re, -im]
                stack = jnp.concatenate(resident + chosen if tile % 2 == 0 else chosen + resident, axis=0)
                where = pl.ds((part * segments + g) * near + tile, LANES, stride=far)
                paired[where, :] = stack.T.astype(jnp.float32)
        return 0

    lax.fori_loop(0, segments, arrange, 0, unroll=4)
    low = lax.broadcasted_iota(jnp.int32, (depth, LANES), 1) < half
    column = lax.broadcasted_iota(jnp.int32, (count, tiles * depth), 1)
    even = lax.rem(lax.div(column, depth), 2) == 0
    none = jnp.zeros((), jnp.bfloat16)
    zeros = jnp.zeros((depth, LANES), jnp.bfloat16)

    def multiply(q, _):
        parts = [
            paired[pl.ds(q * far + tile, depth, stride=near), :].astype(jnp.bfloat16) for tile in range(tiles)
        ]
        turned = jnp.concatenate(parts, axis=0).T
        left = jnp.where(even, turned[half:], turned[:half])
        right = []
        for tile in range(tiles):
            kept = jnp.where(low if tile % 2 == 0 else ~low, parts[tile], none)
            blocks = [zeros] * (tiles // 2)
            blocks[tile // 2] = kept
            right.append(jnp.concatenate(blocks, axis=1))
        result = jnp.dot(left, jnp.concatenate(right, axis=0), preferred_element_type=jnp.float32)
        for h in range(tiles // 2):
            products[pl.ds(q * far_out + h, count, stride=near_out), :] = result[:, h * LANES : (h + 1) * LANES]
        return 0

    lax.fori_loop(0, LANES, multiply, 0, unroll=unroll)
    square = (stations, stations)
    diagonal = lax.broadcasted_iota(jnp.int32, square, 0) == lax.broadcasted_iota(jnp.int32, square, 1)
    turns = count // group

    def place(n):
        return lax.div(n, block // group), pl.multiple_of(lax.rem(n, block // group) * group, group)

    def send(n):
        step, start = place(n)
        slot = lax.rem(n, 2)
        return pltpu.make_async_copy(ready.at[slot], out_ref.at[step, pl.ds(start, group)], sems.at[slot])

    def finish(n, _):
        step, start = place(n)
        for j in range(group):
            row = (step ^ mine) * block + order_ref[step, start + j]
            for h in range(tiles // 2):
                turned = products[pl.ds(row * near_out + h, LANES, stride=far_out), :].astype(jnp.bfloat16).T
                for tile in range(2):
                    for part in range(2):
                        at = (2 * tile + part) * stations
                        lane = part * bins + (2 * h + tile) * LANES
                        cross[j * stations : (j + 1) * stations, lane : lane + LANES] = turned[at : at + stations]
        lagged = jnp.dot(cross[...], inverse_ref[...], preferred_element_type=jnp.float32)
        valid = valid_ref[step, pl.ds(start, group), :].astype(jnp.float32)

        @pl.when(n >= 2)
        def _():
            send(n - 2).wait()

        slot = lax.rem(n, 2)
        for j in range(group):
            kept = jnp.sum(
                jnp.where(diagonal, jnp.broadcast_to(valid[j : j + 1], square), 0.0), axis=1, keepdims=True
            )
            ready[slot, j] = lagged[j * stations : (j + 1) * stations] * kept
        send(n).start()
        return 0

    lax.fori_loop(0, turns, finish, 0)
    for n in range(max(turns - 2, 0), turns):
        send(n).wait()


def correlate(mine, order, valid, own, first, second, inverse):
    segments, stations, width = own.shape
    steps, block = order.shape
    count = steps * block
    lags = inverse.shape[1]
    tiles = width // 2 // LANES
    depth = 2 * segments
    assert steps == 2 and tiles * depth == LANES and 2 * stations == count and 4 * stations == LANES
    group = block
    near, near_out = tiles + 1, tiles // 2 + 1
    pitch = (near, near * depth + 1), (near_out, near_out * count + 1)
    vmem, smem = pl.BlockSpec(memory_space=pltpu.VMEM), pl.BlockSpec(memory_space=pltpu.SMEM)
    return pl.pallas_call(
        functools.partial(correlate_body, group=group, unroll=64, pitch=pitch),
        out_shape=jax.ShapeDtypeStruct((steps, block, stations, lags), jnp.float32),
        in_specs=[smem] * 2 + [vmem] * 5,
        out_specs=pl.BlockSpec(memory_space=pl.ANY),
        scratch_shapes=[
            pltpu.VMEM((LANES * pitch[0][1], LANES), jnp.float32),
            pltpu.VMEM((LANES * pitch[1][1], LANES), jnp.float32),
            pltpu.VMEM((group * stations, width), jnp.bfloat16),
            pltpu.VMEM((2, group, stations, lags), jnp.float32),
            pltpu.SemaphoreType.DMA((2,)),
        ],
        compiler_params=pltpu.CompilerParams(vmem_limit_bytes=33 * 2**20),
        cost_estimate=pl.CostEstimate(
            flops=10**10,
            bytes_accessed=(own.size + first.size + second.size) * 2 + count * stations * lags * 4,
            transcendentals=0,
        ),
    )(mine, order, valid, own, first, second, inverse)


def swap(block, axis, distance):
    count = lax.axis_size(axis)
    return lax.ppermute(block, axis, [(i, i ^ distance) for i in range(count)])


def local(records, filter_taps, ref_owner, reference_station_order, pair_valid):
    axis = "sta"
    devices = lax.axis_size(axis)
    index = lax.axis_index(axis).astype(jnp.int32)
    stations = records.shape[0] // devices
    width = records.shape[1]

    wanted = pick(ref_owner, records, stations)
    held, offsets = [wanted[None]], [0]
    distance = devices
    while distance > 2:
        radix = 4 if distance >= 16 else 2
        distance //= radix
        block = jnp.concatenate(held, axis=0)
        held = [block] + [swap(block, axis, j * distance) for j in range(1, radix)]
        offsets = [j * distance | o for j in range(radix) for o in offsets]
    mine = lax.rem(index, 2)
    of_step = lambda k: jnp.concatenate([lax.dynamic_index_in_dim(part, k, 1, keepdims=False) for part in held], axis=0)
    kept = of_step(mine)
    taken = swap(of_step(1 - mine), axis, 1)

    rows = lax.all_to_all(records.reshape(devices, stations, width), axis, split_axis=0, concat_axis=0)

    band = band_matrix(filter_taps)
    forward = fetch(jnp.asarray(forward_matrix(NFFT)))
    inverse = jnp.asarray(inverse_transform_matrix(NFFT, LAGS, devices * width // NFFT))
    first = whiten([kept, taken], [offsets, [o | 1 for o in offsets]], index[None], band, forward)
    second = swap(first, axis, 1)
    own = whiten([rows], [list(range(devices))], jnp.zeros((1,), jnp.int32), band, forward)
    return correlate(mine[None], reference_station_order, pair_valid, own, first, second, inverse)


def solution(mesh):
    placed = (P("win", "sta"), P(), P("win"), P("win", None), P("win", None, "sta"))
    return jax.shard_map(local, mesh=mesh, in_specs=placed, out_specs=P("win", None, "sta", None), check_vma=False)
```

```python
import functools
import math

import jax
import jax.numpy as jnp
import numpy as np
from jax import lax
from jax.experimental import pallas as pl
from jax.experimental.pallas import tpu as pltpu
from jax.sharding import PartitionSpec as P


NFFT = 1024
LAGS = 256
LANES = 128


def forward_matrix(length):
    time_index = np.arange(length)[:, None]
    bin_index = np.arange(length // 2)[None, :]
    angles = (time_index * bin_index % length).astype(np.float32) * np.float32(2.0 * math.pi / length)
    return np.concatenate([np.cos(angles), -np.sin(angles)], axis=1).astype(jnp.bfloat16)


def inverse_transform_matrix(length, lag_count, segments):
    bin_index = np.arange(length // 2)[:, None]
    shifts = np.arange(lag_count)[None, :] - lag_count // 2
    angles = (bin_index * shifts % length).astype(np.float32) * np.float32(2.0 * math.pi / length)
    factor = np.float32(1.0 / math.sqrt(segments * (length // 2)))
    return np.concatenate([factor * np.cos(angles), -factor * np.sin(angles)], axis=0).astype(jnp.bfloat16)


def pick_body(owner_ref, records_ref, wanted_ref, sems):
    steps, stations, _ = wanted_ref.shape
    copies = []
    for k in range(steps):
        start = pl.multiple_of(owner_ref[k] * stations, stations)
        copies.append(pltpu.make_async_copy(records_ref.at[pl.ds(start, stations)], wanted_ref.at[k], sems.at[k]))
    for copy in copies:
        copy.start()
    for copy in copies:
        copy.wait()


def pick(owner, records, stations):
    steps = owner.shape[0]
    return pl.pallas_call(
        pick_body,
        out_shape=jax.ShapeDtypeStruct((steps, stations, records.shape[1]), records.dtype),
        in_specs=[pl.BlockSpec(memory_space=pltpu.SMEM), pl.BlockSpec(memory_space=pltpu.HBM)],
        out_specs=pl.BlockSpec(memory_space=pltpu.VMEM),
        scratch_shapes=[pltpu.SemaphoreType.DMA((steps,))],
        compiler_params=pltpu.CompilerParams(vmem_limit_bytes=60 * 2**20),
    )(owner, records)


def band_body(row_ref, out_ref):
    width, height = 2 * LANES, 4 * LANES
    rows = jnp.broadcast_to(row_ref[...], (width, height))
    out_ref[...] = pltpu.roll(rows, 0, 1, stride=1, stride_axis=0).T.astype(out_ref.dtype)


def band_matrix(filter_taps):
    count = filter_taps.shape[0]
    before = LANES - (count - 1) // 2
    row = jnp.pad(filter_taps.astype(jnp.float32), (before, 4 * LANES - before - count))[None]
    return pl.pallas_call(
        band_body,
        out_shape=jax.ShapeDtypeStruct((4 * LANES, 2 * LANES), filter_taps.dtype),
        in_specs=[pl.BlockSpec(memory_space=pltpu.VMEM)],
        out_specs=pl.BlockSpec(memory_space=pltpu.VMEM),
        compiler_params=pltpu.CompilerParams(vmem_limit_bytes=4 * 2**20),
    )(row)


def fetch_body(source_ref, out_ref, sem):
    copy = pltpu.make_async_copy(source_ref, out_ref, sem)
    copy.start()
    copy.wait()


def fetch(matrix):
    return pl.pallas_call(
        fetch_body,
        out_shape=jax.ShapeDtypeStruct(matrix.shape, matrix.dtype),
        in_specs=[pl.BlockSpec(memory_space=pltpu.HBM)],
        out_specs=pl.BlockSpec(memory_space=pltpu.VMEM),
        scratch_shapes=[pltpu.SemaphoreType.DMA],
        compiler_params=pltpu.CompilerParams(vmem_limit_bytes=50 * 2**20),
    )(matrix)


def whiten_body(index_ref, *rest, offsets, rows):
    band_ref, forward_ref, out_ref, padded, filtered = rest[-5:]
    stacks = rest[:-5]
    held = [(o, stacks[k].at[i]) for k, some in enumerate(offsets) for i, o in enumerate(some)]
    stations = padded.shape[1]
    width = stacks[0].shape[-1]
    tiles = NFFT // LANES
    parts = width // LANES
    segments = out_ref.shape[0]
    bins = NFFT // 2
    edge = jnp.zeros((stations, LANES), padded.dtype)
    padded[0] = edge
    padded[segments * tiles + 1] = edge
    for offset, piece in held:
        place = 1 + (index_ref[0] ^ offset) * parts
        for part in range(parts):
            padded[place + part] = piece[:, part * LANES : (part + 1) * LANES]
    for first in range(0, segments, rows // stations):
        some = range(first, first + rows // stations)
        for tile in range(0, tiles, 2):
            window = jnp.concatenate(
                [jnp.concatenate([padded[g * tiles + tile + i] for g in some], axis=0) for i in range(4)], axis=1
            )
            filtered[:, tile * LANES : (tile + 2) * LANES] = jnp.dot(
                window, band_ref[...], preferred_element_type=jnp.float32
            ).astype(jnp.bfloat16)
        spectra = jnp.dot(filtered[...], forward_ref[...], preferred_element_type=jnp.float32)
        real_part, imag_part = spectra[:, :bins], spectra[:, bins:]
        energy = real_part * real_part + imag_part * imag_part
        water_level = jnp.sum(energy, axis=-1, keepdims=True) * (1.0 / bins)
        factor = lax.rsqrt(energy + water_level + 1e-06)
        some = slice(first, first + rows // stations)
        out_ref[some, :, :bins] = (real_part * factor).astype(jnp.bfloat16).reshape(-1, stations, bins)
        out_ref[some, :, bins:] = (imag_part * factor).astype(jnp.bfloat16).reshape(-1, stations, bins)


def whiten(raw, offsets, index, band, forward, rows=128):
    _, stations, width = raw[0].shape
    pieces = sum(stack.shape[0] for stack in raw)
    segments = pieces * width // NFFT
    return pl.pallas_call(
        functools.partial(whiten_body, offsets=offsets, rows=rows),
        out_shape=jax.ShapeDtypeStruct((segments, stations, NFFT), jnp.bfloat16),
        in_specs=[pl.BlockSpec(memory_space=pltpu.SMEM)] + [pl.BlockSpec(memory_space=pltpu.VMEM)] * (len(raw) + 2),
        out_specs=pl.BlockSpec(memory_space=pltpu.VMEM),
        scratch_shapes=[
            pltpu.VMEM((segments * NFFT // LANES + 2, stations, LANES), jnp.bfloat16),
            pltpu.VMEM((rows, NFFT), jnp.bfloat16),
        ],
        compiler_params=pltpu.CompilerParams(vmem_limit_bytes=10 * 2**20),
        cost_estimate=pl.CostEstimate(
            flops=2 * segments * stations * NFFT * (NFFT + 512),
            bytes_accessed=2 * segments * stations * NFFT * 2,
            transcendentals=0,
        ),
    )(index, *raw, band, forward)


def correlate_body(
    mine_ref, order_ref, valid_ref, own_ref, first_ref, second_ref, inverse_ref, out_ref, *rest, group, unroll, pitch
):
    paired, products, cross, ready, sems = rest
    segments, stations, width = own_ref.shape
    steps, block = order_ref.shape
    count = steps * block
    bins = width // 2
    tiles = bins // LANES
    depth = 2 * segments
    half = 2 * stations
    (near, far), (near_out, far_out) = pitch
    mine = mine_ref[0]

    def arrange(g, _):
        for tile in range(tiles):
            real = slice(tile * LANES, (tile + 1) * LANES)
            imag = slice(bins + tile * LANES, bins + (tile + 1) * LANES)
            re, im = own_ref[g, :, real], own_ref[g, :, imag]
            for part in range(2):
                lanes = imag if part else real
                chosen = [first_ref[g, :, lanes], second_ref[g, :, lanes]]
                resident = [im, re] if part else [re, -im]
                stack = jnp.concatenate(resident + chosen if tile % 2 == 0 else chosen + resident, axis=0)
                where = pl.ds((part * segments + g) * near + tile, LANES, stride=far)
                paired[where, :] = stack.T.astype(jnp.float32)
        return 0

    lax.fori_loop(0, segments, arrange, 0, unroll=4)
    low = lax.broadcasted_iota(jnp.int32, (depth, LANES), 1) < half
    column = lax.broadcasted_iota(jnp.int32, (count, tiles * depth), 1)
    even = lax.rem(lax.div(column, depth), 2) == 0
    none = jnp.zeros((), jnp.bfloat16)
    zeros = jnp.zeros((depth, LANES), jnp.bfloat16)

    def multiply(q, _):
        parts = [
            paired[pl.ds(q * far + tile, depth, stride=near), :].astype(jnp.bfloat16) for tile in range(tiles)
        ]
        turned = jnp.concatenate(parts, axis=0).T
        left = jnp.where(even, turned[half:], turned[:half])
        right = []
        for tile in range(tiles):
            kept = jnp.where(low if tile % 2 == 0 else ~low, parts[tile], none)
            blocks = [zeros] * (tiles // 2)
            blocks[tile // 2] = kept
            right.append(jnp.concatenate(blocks, axis=1))
        result = jnp.dot(left, jnp.concatenate(right, axis=0), preferred_element_type=jnp.float32)
        for h in range(tiles // 2):
            products[pl.ds(q * far_out + h, count, stride=near_out), :] = result[:, h * LANES : (h + 1) * LANES]
        return 0

    lax.fori_loop(0, LANES, multiply, 0, unroll=unroll)
    square = (stations, stations)
    diagonal = lax.broadcasted_iota(jnp.int32, square, 0) == lax.broadcasted_iota(jnp.int32, square, 1)
    turns = count // group

    def place(n):
        return lax.div(n, block // group), pl.multiple_of(lax.rem(n, block // group) * group, group)

    def send(n):
        step, start = place(n)
        slot = lax.rem(n, 2)
        return pltpu.make_async_copy(ready.at[slot], out_ref.at[step, pl.ds(start, group)], sems.at[slot])

    def finish(n, _):
        step, start = place(n)
        for j in range(group):
            row = (step ^ mine) * block + order_ref[step, start + j]
            for h in range(tiles // 2):
                turned = products[pl.ds(row * near_out + h, LANES, stride=far_out), :].astype(jnp.bfloat16).T
                for tile in range(2):
                    for part in range(2):
                        at = (2 * tile + part) * stations
                        lane = part * bins + (2 * h + tile) * LANES
                        cross[j * stations : (j + 1) * stations, lane : lane + LANES] = turned[at : at + stations]
        lagged = jnp.dot(cross[...], inverse_ref[...], preferred_element_type=jnp.float32)
        valid = valid_ref[step, pl.ds(start, group), :].astype(jnp.float32)

        @pl.when(n >= 2)
        def _():
            send(n - 2).wait()

        slot = lax.rem(n, 2)
        for j in range(group):
            kept = jnp.sum(
                jnp.where(diagonal, jnp.broadcast_to(valid[j : j + 1], square), 0.0), axis=1, keepdims=True
            )
            ready[slot, j] = lagged[j * stations : (j + 1) * stations] * kept
        send(n).start()
        return 0

    lax.fori_loop(0, turns, finish, 0)
    for n in range(max(turns - 2, 0), turns):
        send(n).wait()


def correlate(mine, order, valid, own, first, second, inverse):
    segments, stations, width = own.shape
    steps, block = order.shape
    count = steps * block
    lags = inverse.shape[1]
    tiles = width // 2 // LANES
    depth = 2 * segments
    assert steps == 2 and tiles * depth == LANES and 2 * stations == count and 4 * stations == LANES
    group = block
    near, near_out = tiles + 1, tiles // 2 + 1
    pitch = (near, near * depth + 1), (near_out, near_out * count + 1)
    vmem, smem = pl.BlockSpec(memory_space=pltpu.VMEM), pl.BlockSpec(memory_space=pltpu.SMEM)
    return pl.pallas_call(
        functools.partial(correlate_body, group=group, unroll=64, pitch=pitch),
        out_shape=jax.ShapeDtypeStruct((steps, block, stations, lags), jnp.float32),
        in_specs=[smem] * 2 + [vmem] * 5,
        out_specs=pl.BlockSpec(memory_space=pl.ANY),
        scratch_shapes=[
            pltpu.VMEM((LANES * pitch[0][1], LANES), jnp.float32),
            pltpu.VMEM((LANES * pitch[1][1], LANES), jnp.float32),
            pltpu.VMEM((group * stations, width), jnp.bfloat16),
            pltpu.VMEM((2, group, stations, lags), jnp.float32),
            pltpu.SemaphoreType.DMA((2,)),
        ],
        compiler_params=pltpu.CompilerParams(vmem_limit_bytes=33 * 2**20),
        cost_estimate=pl.CostEstimate(
            flops=10**10,
            bytes_accessed=(own.size + first.size + second.size) * 2 + count * stations * lags * 4,
            transcendentals=0,
        ),
    )(mine, order, valid, own, first, second, inverse)


def swap(block, axis, distance):
    count = lax.axis_size(axis)
    return lax.ppermute(block, axis, [(i, i ^ distance) for i in range(count)])


def local(records, filter_taps, ref_owner, reference_station_order, pair_valid):
    axis = "sta"
    devices = lax.axis_size(axis)
    index = lax.axis_index(axis).astype(jnp.int32)
    stations = records.shape[0] // devices
    width = records.shape[1]

    wanted = pick(ref_owner, records, stations)
    own_piece = wanted[None]
    far_piece = swap(own_piece, axis, devices // 2)
    chains = {"near": (own_piece, [0]), "far": (far_piece, [devices // 2])}
    distance, stage = devices // 4, 0
    while distance > 1:
        for name, (block, offsets) in chains.items():
            block = jnp.concatenate([block, swap(block, axis, distance)], axis=0)
            chains[name] = block, offsets + [distance | o for o in offsets]
        distance //= 2
        stage += 1
    mine = lax.rem(index, 2)
    pieces, offsets = [], []
    for (block, some) in chains.values():
        pieces.append(lax.dynamic_index_in_dim(block, mine, 1, keepdims=False))
        pieces.append(swap(lax.dynamic_index_in_dim(block, 1 - mine, 1, keepdims=False), axis, 1))
        offsets += [some, [o | 1 for o in some]]

    rows = lax.all_to_all(records.reshape(devices, stations, width), axis, split_axis=0, concat_axis=0)

    band = band_matrix(filter_taps)
    forward = fetch(jnp.asarray(forward_matrix(NFFT)))
    inverse = jnp.asarray(inverse_transform_matrix(NFFT, LAGS, devices * width // NFFT))
    first = whiten(pieces, offsets, index[None], band, forward)
    second = swap(first, axis, 1)
    own = whiten([rows], [list(range(devices))], jnp.zeros((1,), jnp.int32), band, forward)
    return correlate(mine[None], reference_station_order, pair_valid, own, first, second, inverse)


def solution(mesh):
    placed = (P("win", "sta"), P(), P("win"), P("win", None), P("win", None, "sta"))
    return jax.shard_map(local, mesh=mesh, in_specs=placed, out_specs=P("win", None, "sta", None), check_vma=False)
```

```python
import functools
import math

import jax
import jax.numpy as jnp
import numpy as np
from jax import lax
from jax.experimental import pallas as pl
from jax.experimental.pallas import tpu as pltpu
from jax.sharding import PartitionSpec as P


NFFT = 1024
LAGS = 256
LANES = 128


def forward_matrix(length):
    time_index = np.arange(length)[:, None]
    bin_index = np.arange(length // 2)[None, :]
    angles = (time_index * bin_index % length).astype(np.float32) * np.float32(2.0 * math.pi / length)
    return np.concatenate([np.cos(angles), -np.sin(angles)], axis=1).astype(jnp.bfloat16)


def inverse_transform_matrix(length, lag_count, segments):
    bin_index = np.arange(length // 2)[:, None]
    shifts = np.arange(lag_count)[None, :] - lag_count // 2
    angles = (bin_index * shifts % length).astype(np.float32) * np.float32(2.0 * math.pi / length)
    factor = np.float32(1.0 / math.sqrt(segments * (length // 2)))
    return np.concatenate([factor * np.cos(angles), -factor * np.sin(angles)], axis=0).astype(jnp.bfloat16)


def pick_body(owner_ref, records_ref, wanted_ref, sems):
    steps, stations, _ = wanted_ref.shape
    copies = []
    for k in range(steps):
        start = pl.multiple_of(owner_ref[k] * stations, stations)
        copies.append(pltpu.make_async_copy(records_ref.at[pl.ds(start, stations)], wanted_ref.at[k], sems.at[k]))
    for copy in copies:
        copy.start()
    for copy in copies:
        copy.wait()


def pick(owner, records, stations):
    steps = owner.shape[0]
    return pl.pallas_call(
        pick_body,
        out_shape=jax.ShapeDtypeStruct((steps, stations, records.shape[1]), records.dtype),
        in_specs=[pl.BlockSpec(memory_space=pltpu.SMEM), pl.BlockSpec(memory_space=pltpu.HBM)],
        out_specs=pl.BlockSpec(memory_space=pltpu.VMEM),
        scratch_shapes=[pltpu.SemaphoreType.DMA((steps,))],
        compiler_params=pltpu.CompilerParams(vmem_limit_bytes=60 * 2**20),
    )(owner, records)


def band_body(row_ref, out_ref):
    width, height = 2 * LANES, 4 * LANES
    rows = jnp.broadcast_to(row_ref[...], (width, height))
    out_ref[...] = pltpu.roll(rows, 0, 1, stride=1, stride_axis=0).T.astype(out_ref.dtype)


def band_matrix(filter_taps):
    count = filter_taps.shape[0]
    before = LANES - (count - 1) // 2
    row = jnp.pad(filter_taps.astype(jnp.float32), (before, 4 * LANES - before - count))[None]
    return pl.pallas_call(
        band_body,
        out_shape=jax.ShapeDtypeStruct((4 * LANES, 2 * LANES), filter_taps.dtype),
        in_specs=[pl.BlockSpec(memory_space=pltpu.VMEM)],
        out_specs=pl.BlockSpec(memory_space=pltpu.VMEM),
        compiler_params=pltpu.CompilerParams(vmem_limit_bytes=4 * 2**20),
    )(row)


def fetch_body(source_ref, out_ref, sem):
    copy = pltpu.make_async_copy(source_ref, out_ref, sem)
    copy.start()
    copy.wait()


def fetch(matrix):
    return pl.pallas_call(
        fetch_body,
        out_shape=jax.ShapeDtypeStruct(matrix.shape, matrix.dtype),
        in_specs=[pl.BlockSpec(memory_space=pltpu.HBM)],
        out_specs=pl.BlockSpec(memory_space=pltpu.VMEM),
        scratch_shapes=[pltpu.SemaphoreType.DMA],
        compiler_params=pltpu.CompilerParams(vmem_limit_bytes=50 * 2**20),
    )(matrix)


def whiten_body(index_ref, *rest, offsets, rows):
    band_ref, forward_ref, out_ref, padded, filtered = rest[-5:]
    stacks = rest[:-5]
    held = [(o, stacks[k].at[i]) for k, some in enumerate(offsets) for i, o in enumerate(some)]
    stations = padded.shape[1]
    width = stacks[0].shape[-1]
    tiles = NFFT // LANES
    parts = width // LANES
    segments = out_ref.shape[0]
    bins = NFFT // 2
    edge = jnp.zeros((stations, LANES), padded.dtype)
    padded[0] = edge
    padded[segments * tiles + 1] = edge
    for offset, piece in held:
        place = 1 + (index_ref[0] ^ offset) * parts
        for part in range(parts):
            padded[place + part] = piece[:, part * LANES : (part + 1) * LANES]
    for first in range(0, segments, rows // stations):
        some = range(first, first + rows // stations)
        for tile in range(0, tiles, 2):
            window = jnp.concatenate(
                [jnp.concatenate([padded[g * tiles + tile + i] for g in some], axis=0) for i in range(4)], axis=1
            )
            filtered[:, tile * LANES : (tile + 2) * LANES] = jnp.dot(
                window, band_ref[...], preferred_element_type=jnp.float32
            ).astype(jnp.bfloat16)
        spectra = jnp.dot(filtered[...], forward_ref[...], preferred_element_type=jnp.float32)
        real_part, imag_part = spectra[:, :bins], spectra[:, bins:]
        energy = real_part * real_part + imag_part * imag_part
        water_level = jnp.sum(energy, axis=-1, keepdims=True) * (1.0 / bins)
        factor = lax.rsqrt(energy + water_level + 1e-06)
        some = slice(first, first + rows // stations)
        out_ref[some, :, :bins] = (real_part * factor).astype(jnp.bfloat16).reshape(-1, stations, bins)
        out_ref[some, :, bins:] = (imag_part * factor).astype(jnp.bfloat16).reshape(-1, stations, bins)


def whiten(raw, offsets, index, band, forward, rows=128):
    _, stations, width = raw[0].shape
    pieces = sum(stack.shape[0] for stack in raw)
    segments = pieces * width // NFFT
    return pl.pallas_call(
        functools.partial(whiten_body, offsets=offsets, rows=rows),
        out_shape=jax.ShapeDtypeStruct((segments, stations, NFFT), jnp.bfloat16),
        in_specs=[pl.BlockSpec(memory_space=pltpu.SMEM)] + [pl.BlockSpec(memory_space=pltpu.VMEM)] * (len(raw) + 2),
        out_specs=pl.BlockSpec(memory_space=pltpu.VMEM),
        scratch_shapes=[
            pltpu.VMEM((segments * NFFT // LANES + 2, stations, LANES), jnp.bfloat16),
            pltpu.VMEM((rows, NFFT), jnp.bfloat16),
        ],
        compiler_params=pltpu.CompilerParams(vmem_limit_bytes=10 * 2**20),
        cost_estimate=pl.CostEstimate(
            flops=2 * segments * stations * NFFT * (NFFT + 512),
            bytes_accessed=2 * segments * stations * NFFT * 2,
            transcendentals=0,
        ),
    )(index, *raw, band, forward)


def correlate_body(
    mine_ref, order_ref, valid_ref, own_ref, first_ref, second_ref, inverse_ref, out_ref, *rest, group, unroll, pitch
):
    paired, products, cross, ready, sems = rest
    segments, stations, width = own_ref.shape
    steps, block = order_ref.shape
    count = steps * block
    bins = width // 2
    tiles = bins // LANES
    depth = 2 * segments
    half = 2 * stations
    (near, far), (near_out, far_out) = pitch
    mine = mine_ref[0]

    def arrange(g, _):
        for tile in range(tiles):
            real = slice(tile * LANES, (tile + 1) * LANES)
            imag = slice(bins + tile * LANES, bins + (tile + 1) * LANES)
            re, im = own_ref[g, :, real], own_ref[g, :, imag]
            for part in range(2):
                lanes = imag if part else real
                chosen = [first_ref[g, :, lanes], second_ref[g, :, lanes]]
                resident = [im, re] if part else [re, -im]
                stack = jnp.concatenate(resident + chosen if tile % 2 == 0 else chosen + resident, axis=0)
                where = pl.ds((part * segments + g) * near + tile, LANES, stride=far)
                paired[where, :] = stack.T.astype(jnp.float32)
        return 0

    lax.fori_loop(0, segments, arrange, 0, unroll=4)
    low = lax.broadcasted_iota(jnp.int32, (depth, LANES), 1) < half
    column = lax.broadcasted_iota(jnp.int32, (count, tiles * depth), 1)
    even = lax.rem(lax.div(column, depth), 2) == 0
    none = jnp.zeros((), jnp.bfloat16)
    zeros = jnp.zeros((depth, LANES), jnp.bfloat16)

    def multiply(q, _):
        parts = [
            paired[pl.ds(q * far + tile, depth, stride=near), :].astype(jnp.bfloat16) for tile in range(tiles)
        ]
        turned = jnp.concatenate(parts, axis=0).T
        left = jnp.where(even, turned[half:], turned[:half])
        right = []
        for tile in range(tiles):
            kept = jnp.where(low if tile % 2 == 0 else ~low, parts[tile], none)
            blocks = [zeros] * (tiles // 2)
            blocks[tile // 2] = kept
            right.append(jnp.concatenate(blocks, axis=1))
        result = jnp.dot(left, jnp.concatenate(right, axis=0), preferred_element_type=jnp.float32)
        for h in range(tiles // 2):
            products[pl.ds(q * far_out + h, count, stride=near_out), :] = result[:, h * LANES : (h + 1) * LANES]
        return 0

    lax.fori_loop(0, LANES, multiply, 0, unroll=unroll)
    square = (stations, stations)
    diagonal = lax.broadcasted_iota(jnp.int32, square, 0) == lax.broadcasted_iota(jnp.int32, square, 1)
    turns = count // group

    def place(n):
        return lax.div(n, block // group), pl.multiple_of(lax.rem(n, block // group) * group, group)

    def send(n):
        step, start = place(n)
        slot = lax.rem(n, 2)
        return pltpu.make_async_copy(ready.at[slot], out_ref.at[step, pl.ds(start, group)], sems.at[slot])

    def finish(n, _):
        step, start = place(n)
        for j in range(group):
            row = (step ^ mine) * block + order_ref[step, start + j]
            for h in range(tiles // 2):
                turned = products[pl.ds(row * near_out + h, LANES, stride=far_out), :].astype(jnp.bfloat16).T
                for tile in range(2):
                    for part in range(2):
                        at = (2 * tile + part) * stations
                        lane = part * bins + (2 * h + tile) * LANES
                        cross[j * stations : (j + 1) * stations, lane : lane + LANES] = turned[at : at + stations]
        lagged = jnp.dot(cross[...], inverse_ref[...], preferred_element_type=jnp.float32)
        valid = valid_ref[step, pl.ds(start, group), :].astype(jnp.float32)

        @pl.when(n >= 2)
        def _():
            send(n - 2).wait()

        slot = lax.rem(n, 2)
        for j in range(group):
            kept = jnp.sum(
                jnp.where(diagonal, jnp.broadcast_to(valid[j : j + 1], square), 0.0), axis=1, keepdims=True
            )
            ready[slot, j] = lagged[j * stations : (j + 1) * stations] * kept
        send(n).start()
        return 0

    lax.fori_loop(0, turns, finish, 0)
    for n in range(max(turns - 2, 0), turns):
        send(n).wait()


def correlate(mine, order, valid, own, first, second, inverse):
    segments, stations, width = own.shape
    steps, block = order.shape
    count = steps * block
    lags = inverse.shape[1]
    tiles = width // 2 // LANES
    depth = 2 * segments
    assert steps == 2 and tiles * depth == LANES and 2 * stations == count and 4 * stations == LANES
    group = block
    near, near_out = tiles + 1, tiles // 2 + 1
    pitch = (near, near * depth + 1), (near_out, near_out * count + 1)
    vmem, smem = pl.BlockSpec(memory_space=pltpu.VMEM), pl.BlockSpec(memory_space=pltpu.SMEM)
    return pl.pallas_call(
        functools.partial(correlate_body, group=group, unroll=64, pitch=pitch),
        out_shape=jax.ShapeDtypeStruct((steps, block, stations, lags), jnp.float32),
        in_specs=[smem] * 2 + [vmem] * 5,
        out_specs=pl.BlockSpec(memory_space=pl.ANY),
        scratch_shapes=[
            pltpu.VMEM((LANES * pitch[0][1], LANES), jnp.float32),
            pltpu.VMEM((LANES * pitch[1][1], LANES), jnp.float32),
            pltpu.VMEM((group * stations, width), jnp.bfloat16),
            pltpu.VMEM((2, group, stations, lags), jnp.float32),
            pltpu.SemaphoreType.DMA((2,)),
        ],
        compiler_params=pltpu.CompilerParams(vmem_limit_bytes=33 * 2**20),
        cost_estimate=pl.CostEstimate(
            flops=10**10,
            bytes_accessed=(own.size + first.size + second.size) * 2 + count * stations * lags * 4,
            transcendentals=0,
        ),
    )(mine, order, valid, own, first, second, inverse)


def swap(block, axis, distance):
    count = lax.axis_size(axis)
    return lax.ppermute(block, axis, [(i, i ^ distance) for i in range(count)])


def local(records, filter_taps, ref_owner, reference_station_order, pair_valid):
    axis = "sta"
    devices = lax.axis_size(axis)
    index = lax.axis_index(axis).astype(jnp.int32)
    stations = records.shape[0] // devices
    width = records.shape[1]

    wanted = pick(ref_owner, records, stations)
    own_piece = wanted[None]
    quarter = devices // 4
    crossed = [swap(own_piece, axis, j * quarter) for j in range(1, 4)]
    chains = {
        "near": (jnp.concatenate([own_piece, crossed[0]], axis=0), [0, quarter]),
        "far": (jnp.concatenate(crossed[1:], axis=0), [2 * quarter, 3 * quarter]),
    }
    distance, stage = devices // 8, 0
    while distance > 1:
        for name, (block, offsets) in chains.items():
            block = jnp.concatenate([block, swap(block, axis, distance)], axis=0)
            chains[name] = block, offsets + [distance | o for o in offsets]
        distance //= 2
        stage += 1
    mine = lax.rem(index, 2)
    pieces, offsets = [], []
    for (block, some) in chains.values():
        pieces.append(lax.dynamic_index_in_dim(block, mine, 1, keepdims=False))
        pieces.append(swap(lax.dynamic_index_in_dim(block, 1 - mine, 1, keepdims=False), axis, 1))
        offsets += [some, [o | 1 for o in some]]

    rows = lax.all_to_all(records.reshape(devices, stations, width), axis, split_axis=0, concat_axis=0)

    band = band_matrix(filter_taps)
    forward = fetch(jnp.asarray(forward_matrix(NFFT)))
    inverse = jnp.asarray(inverse_transform_matrix(NFFT, LAGS, devices * width // NFFT))
    first = whiten(pieces, offsets, index[None], band, forward)
    second = swap(first, axis, 1)
    own = whiten([rows], [list(range(devices))], jnp.zeros((1,), jnp.int32), band, forward)
    return correlate(mine[None], reference_station_order, pair_valid, own, first, second, inverse)


def solution(mesh):
    placed = (P("win", "sta"), P(), P("win"), P("win", None), P("win", None, "sta"))
    return jax.shard_map(local, mesh=mesh, in_specs=placed, out_specs=P("win", None, "sta", None), check_vma=False)
```

```python
import functools
import math

import jax
import jax.numpy as jnp
import numpy as np
from jax import lax
from jax.experimental import pallas as pl
from jax.experimental.pallas import tpu as pltpu
from jax.sharding import PartitionSpec as P


NFFT = 1024
LAGS = 256
LANES = 128


def forward_matrix(length):
    time_index = np.arange(length)[:, None]
    bin_index = np.arange(length // 2)[None, :]
    angles = (time_index * bin_index % length).astype(np.float32) * np.float32(2.0 * math.pi / length)
    return np.concatenate([np.cos(angles), -np.sin(angles)], axis=1).astype(jnp.bfloat16)


def inverse_transform_matrix(length, lag_count, segments):
    bin_index = np.arange(length // 2)[:, None]
    shifts = np.arange(lag_count)[None, :] - lag_count // 2
    angles = (bin_index * shifts % length).astype(np.float32) * np.float32(2.0 * math.pi / length)
    factor = np.float32(1.0 / math.sqrt(segments * (length // 2)))
    return np.concatenate([factor * np.cos(angles), -factor * np.sin(angles)], axis=0).astype(jnp.bfloat16)


def pick_body(owner_ref, records_ref, wanted_ref, sems):
    steps, stations, _ = wanted_ref.shape
    copies = []
    for k in range(steps):
        start = pl.multiple_of(owner_ref[k] * stations, stations)
        copies.append(pltpu.make_async_copy(records_ref.at[pl.ds(start, stations)], wanted_ref.at[k], sems.at[k]))
    for copy in copies:
        copy.start()
    for copy in copies:
        copy.wait()


def pick(owner, records, stations):
    steps = owner.shape[0]
    return pl.pallas_call(
        pick_body,
        out_shape=jax.ShapeDtypeStruct((steps, stations, records.shape[1]), records.dtype),
        in_specs=[pl.BlockSpec(memory_space=pltpu.SMEM), pl.BlockSpec(memory_space=pltpu.HBM)],
        out_specs=pl.BlockSpec(memory_space=pltpu.VMEM),
        scratch_shapes=[pltpu.SemaphoreType.DMA((steps,))],
        compiler_params=pltpu.CompilerParams(vmem_limit_bytes=60 * 2**20),
    )(owner, records)


def band_body(row_ref, out_ref):
    width, height = 2 * LANES, 4 * LANES
    rows = jnp.broadcast_to(row_ref[...], (width, height))
    out_ref[...] = pltpu.roll(rows, 0, 1, stride=1, stride_axis=0).T.astype(out_ref.dtype)


def band_matrix(filter_taps):
    count = filter_taps.shape[0]
    before = LANES - (count - 1) // 2
    row = jnp.pad(filter_taps.astype(jnp.float32), (before, 4 * LANES - before - count))[None]
    return pl.pallas_call(
        band_body,
        out_shape=jax.ShapeDtypeStruct((4 * LANES, 2 * LANES), filter_taps.dtype),
        in_specs=[pl.BlockSpec(memory_space=pltpu.VMEM)],
        out_specs=pl.BlockSpec(memory_space=pltpu.VMEM),
        compiler_params=pltpu.CompilerParams(vmem_limit_bytes=4 * 2**20),
    )(row)


def fetch_body(source_ref, out_ref, sem):
    copy = pltpu.make_async_copy(source_ref, out_ref, sem)
    copy.start()
    copy.wait()


def fetch(matrix):
    return pl.pallas_call(
        fetch_body,
        out_shape=jax.ShapeDtypeStruct(matrix.shape, matrix.dtype),
        in_specs=[pl.BlockSpec(memory_space=pltpu.HBM)],
        out_specs=pl.BlockSpec(memory_space=pltpu.VMEM),
        scratch_shapes=[pltpu.SemaphoreType.DMA],
        compiler_params=pltpu.CompilerParams(vmem_limit_bytes=50 * 2**20),
    )(matrix)


def whiten_body(index_ref, *rest, offsets, rows):
    band_ref, forward_ref, out_ref, padded, filtered = rest[-5:]
    stacks = rest[:-5]
    held = [(o, stacks[k].at[i]) for k, some in enumerate(offsets) for i, o in enumerate(some)]
    stations = padded.shape[1]
    width = stacks[0].shape[-1]
    tiles = NFFT // LANES
    parts = width // LANES
    segments = out_ref.shape[0]
    bins = NFFT // 2
    edge = jnp.zeros((stations, LANES), padded.dtype)
    padded[0] = edge
    padded[segments * tiles + 1] = edge
    for offset, piece in held:
        place = 1 + (index_ref[0] ^ offset) * parts
        for part in range(parts):
            padded[place + part] = piece[:, part * LANES : (part + 1) * LANES]
    for first in range(0, segments, rows // stations):
        some = range(first, first + rows // stations)
        for tile in range(0, tiles, 2):
            window = jnp.concatenate(
                [jnp.concatenate([padded[g * tiles + tile + i] for g in some], axis=0) for i in range(4)], axis=1
            )
            filtered[:, tile * LANES : (tile + 2) * LANES] = jnp.dot(
                window, band_ref[...], preferred_element_type=jnp.float32
            ).astype(jnp.bfloat16)
        spectra = jnp.dot(filtered[...], forward_ref[...], preferred_element_type=jnp.float32)
        real_part, imag_part = spectra[:, :bins], spectra[:, bins:]
        energy = real_part * real_part + imag_part * imag_part
        water_level = jnp.sum(energy, axis=-1, keepdims=True) * (1.0 / bins)
        factor = lax.rsqrt(energy + water_level + 1e-06)
        some = slice(first, first + rows // stations)
        out_ref[some, :, :bins] = (real_part * factor).astype(jnp.bfloat16).reshape(-1, stations, bins)
        out_ref[some, :, bins:] = (imag_part * factor).astype(jnp.bfloat16).reshape(-1, stations, bins)


def whiten(raw, offsets, index, band, forward, rows=128):
    _, stations, width = raw[0].shape
    pieces = sum(stack.shape[0] for stack in raw)
    segments = pieces * width // NFFT
    return pl.pallas_call(
        functools.partial(whiten_body, offsets=offsets, rows=rows),
        out_shape=jax.ShapeDtypeStruct((segments, stations, NFFT), jnp.bfloat16),
        in_specs=[pl.BlockSpec(memory_space=pltpu.SMEM)] + [pl.BlockSpec(memory_space=pltpu.VMEM)] * (len(raw) + 2),
        out_specs=pl.BlockSpec(memory_space=pltpu.VMEM),
        scratch_shapes=[
            pltpu.VMEM((segments * NFFT // LANES + 2, stations, LANES), jnp.bfloat16),
            pltpu.VMEM((rows, NFFT), jnp.bfloat16),
        ],
        compiler_params=pltpu.CompilerParams(vmem_limit_bytes=10 * 2**20),
        cost_estimate=pl.CostEstimate(
            flops=2 * segments * stations * NFFT * (NFFT + 512),
            bytes_accessed=2 * segments * stations * NFFT * 2,
            transcendentals=0,
        ),
    )(index, *raw, band, forward)


def correlate_body(
    mine_ref, order_ref, valid_ref, own_ref, first_ref, second_ref, inverse_ref, out_ref, *rest, group, unroll, pitch
):
    paired, products, cross, ready, sems = rest
    segments, stations, width = own_ref.shape
    steps, block = order_ref.shape
    count = steps * block
    bins = width // 2
    tiles = bins // LANES
    depth = 2 * segments
    half = 2 * stations
    (near, far), (near_out, far_out) = pitch
    mine = mine_ref[0]

    def arrange(g, _):
        for tile in range(tiles):
            real = slice(tile * LANES, (tile + 1) * LANES)
            imag = slice(bins + tile * LANES, bins + (tile + 1) * LANES)
            re, im = own_ref[g, :, real], own_ref[g, :, imag]
            for part in range(2):
                lanes = imag if part else real
                chosen = [first_ref[g, :, lanes], second_ref[g, :, lanes]]
                resident = [im, re] if part else [re, -im]
                stack = jnp.concatenate(resident + chosen if tile % 2 == 0 else chosen + resident, axis=0)
                where = pl.ds((part * segments + g) * near + tile, LANES, stride=far)
                paired[where, :] = stack.T.astype(jnp.float32)
        return 0

    lax.fori_loop(0, segments, arrange, 0, unroll=4)
    low = lax.broadcasted_iota(jnp.int32, (depth, LANES), 1) < half
    column = lax.broadcasted_iota(jnp.int32, (count, tiles * depth), 1)
    even = lax.rem(lax.div(column, depth), 2) == 0
    none = jnp.zeros((), jnp.bfloat16)
    zeros = jnp.zeros((depth, LANES), jnp.bfloat16)

    def multiply(q, _):
        parts = [
            paired[pl.ds(q * far + tile, depth, stride=near), :].astype(jnp.bfloat16) for tile in range(tiles)
        ]
        turned = jnp.concatenate(parts, axis=0).T
        left = jnp.where(even, turned[half:], turned[:half])
        right = []
        for tile in range(tiles):
            kept = jnp.where(low if tile % 2 == 0 else ~low, parts[tile], none)
            blocks = [zeros] * (tiles // 2)
            blocks[tile // 2] = kept
            right.append(jnp.concatenate(blocks, axis=1))
        result = jnp.dot(left, jnp.concatenate(right, axis=0), preferred_element_type=jnp.float32)
        for h in range(tiles // 2):
            products[pl.ds(q * far_out + h, count, stride=near_out), :] = result[:, h * LANES : (h + 1) * LANES]
        return 0

    lax.fori_loop(0, LANES, multiply, 0, unroll=unroll)
    square = (stations, stations)
    diagonal = lax.broadcasted_iota(jnp.int32, square, 0) == lax.broadcasted_iota(jnp.int32, square, 1)
    turns = count // group

    def place(n):
        return lax.div(n, block // group), pl.multiple_of(lax.rem(n, block // group) * group, group)

    def send(n):
        step, start = place(n)
        slot = lax.rem(n, 2)
        return pltpu.make_async_copy(ready.at[slot], out_ref.at[step, pl.ds(start, group)], sems.at[slot])

    def finish(n, _):
        step, start = place(n)
        for j in range(group):
            row = (step ^ mine) * block + order_ref[step, start + j]
            for h in range(tiles // 2):
                turned = products[pl.ds(row * near_out + h, LANES, stride=far_out), :].astype(jnp.bfloat16).T
                for tile in range(2):
                    for part in range(2):
                        at = (2 * tile + part) * stations
                        lane = part * bins + (2 * h + tile) * LANES
                        cross[j * stations : (j + 1) * stations, lane : lane + LANES] = turned[at : at + stations]
        lagged = jnp.dot(cross[...], inverse_ref[...], preferred_element_type=jnp.float32)
        valid = valid_ref[step, pl.ds(start, group), :].astype(jnp.float32)

        @pl.when(n >= 2)
        def _():
            send(n - 2).wait()

        slot = lax.rem(n, 2)
        for j in range(group):
            kept = jnp.sum(
                jnp.where(diagonal, jnp.broadcast_to(valid[j : j + 1], square), 0.0), axis=1, keepdims=True
            )
            ready[slot, j] = lagged[j * stations : (j + 1) * stations] * kept
        send(n).start()
        return 0

    lax.fori_loop(0, turns, finish, 0)
    for n in range(max(turns - 2, 0), turns):
        send(n).wait()


def correlate(mine, order, valid, own, first, second, inverse):
    segments, stations, width = own.shape
    steps, block = order.shape
    count = steps * block
    lags = inverse.shape[1]
    tiles = width // 2 // LANES
    depth = 2 * segments
    assert steps == 2 and tiles * depth == LANES and 2 * stations == count and 4 * stations == LANES
    group = block
    near, near_out = tiles + 1, tiles // 2 + 1
    pitch = (near, near * depth + 1), (near_out, near_out * count + 1)
    vmem, smem = pl.BlockSpec(memory_space=pltpu.VMEM), pl.BlockSpec(memory_space=pltpu.SMEM)
    return pl.pallas_call(
        functools.partial(correlate_body, group=group, unroll=64, pitch=pitch),
        out_shape=jax.ShapeDtypeStruct((steps, block, stations, lags), jnp.float32),
        in_specs=[smem] * 2 + [vmem] * 5,
        out_specs=pl.BlockSpec(memory_space=pl.ANY),
        scratch_shapes=[
            pltpu.VMEM((LANES * pitch[0][1], LANES), jnp.float32),
            pltpu.VMEM((LANES * pitch[1][1], LANES), jnp.float32),
            pltpu.VMEM((group * stations, width), jnp.bfloat16),
            pltpu.VMEM((2, group, stations, lags), jnp.float32),
            pltpu.SemaphoreType.DMA((2,)),
        ],
        compiler_params=pltpu.CompilerParams(vmem_limit_bytes=33 * 2**20),
        cost_estimate=pl.CostEstimate(
            flops=10**10,
            bytes_accessed=(own.size + first.size + second.size) * 2 + count * stations * lags * 4,
            transcendentals=0,
        ),
    )(mine, order, valid, own, first, second, inverse)


def swap(block, axis, distance):
    count = lax.axis_size(axis)
    return lax.ppermute(block, axis, [(i, i ^ distance) for i in range(count)])


def local(records, filter_taps, ref_owner, reference_station_order, pair_valid):
    axis = "sta"
    devices = lax.axis_size(axis)
    index = lax.axis_index(axis).astype(jnp.int32)
    stations = records.shape[0] // devices
    width = records.shape[1]

    wanted = pick(ref_owner, records, stations)
    own_piece = wanted[None]
    quarter = devices // 4
    quarter_of = lambda source, target: [(source * quarter + i, target * quarter + i) for i in range(quarter)]
    beside = swap(own_piece, axis, quarter)
    inner = lax.ppermute(own_piece, axis, quarter_of(1, 2) + quarter_of(2, 1))
    outer = lax.ppermute(own_piece, axis, quarter_of(0, 2) + quarter_of(3, 1))
    both = jnp.concatenate([inner, outer], axis=0)
    relayed = lax.ppermute(both, axis, quarter_of(1, 0) + quarter_of(2, 3))
    place = index // quarter
    far_block = jnp.where((place == 1) | (place == 2), both, relayed[::-1])
    chains = {
        "near": (jnp.concatenate([own_piece, beside], axis=0), [0, quarter]),
        "far": (far_block, [3 * quarter, 2 * quarter]),
    }
    distance, stage = devices // 8, 0
    while distance > 1:
        for name, (block, offsets) in chains.items():
            block = jnp.concatenate([block, swap(block, axis, distance)], axis=0)
            chains[name] = block, offsets + [distance | o for o in offsets]
        distance //= 2
        stage += 1
    mine = lax.rem(index, 2)
    pieces, offsets = [], []
    for (block, some) in chains.values():
        pieces.append(lax.dynamic_index_in_dim(block, mine, 1, keepdims=False))
        pieces.append(swap(lax.dynamic_index_in_dim(block, 1 - mine, 1, keepdims=False), axis, 1))
        offsets += [some, [o | 1 for o in some]]

    rows = lax.all_to_all(records.reshape(devices, stations, width), axis, split_axis=0, concat_axis=0)

    band = band_matrix(filter_taps)
    forward = fetch(jnp.asarray(forward_matrix(NFFT)))
    inverse = jnp.asarray(inverse_transform_matrix(NFFT, LAGS, devices * width // NFFT))
    first = whiten(pieces, offsets, index[None], band, forward)
    second = swap(first, axis, 1)
    own = whiten([rows], [list(range(devices))], jnp.zeros((1,), jnp.int32), band, forward)
    return correlate(mine[None], reference_station_order, pair_valid, own, first, second, inverse)


def solution(mesh):
    placed = (P("win", "sta"), P(), P("win"), P("win", None), P("win", None, "sta"))
    return jax.shard_map(local, mesh=mesh, in_specs=placed, out_specs=P("win", None, "sta", None), check_vma=False)
```

```python
import functools
import math

import jax
import jax.numpy as jnp
import numpy as np
from jax import lax
from jax.experimental import pallas as pl
from jax.experimental.pallas import tpu as pltpu
from jax.sharding import PartitionSpec as P


NFFT = 1024
PIECE = 8
LAGS = 256
LANES = 128


def forward_matrix(length):
    time_index = np.arange(length)[:, None]
    bin_index = np.arange(length // 2)[None, :]
    angles = (time_index * bin_index % length).astype(np.float32) * np.float32(2.0 * math.pi / length)
    return np.concatenate([np.cos(angles), -np.sin(angles)], axis=1).astype(jnp.bfloat16)


def inverse_transform_matrix(length, lag_count, segments):
    bin_index = np.arange(length // 2)[:, None]
    shifts = np.arange(lag_count)[None, :] - lag_count // 2
    angles = (bin_index * shifts % length).astype(np.float32) * np.float32(2.0 * math.pi / length)
    factor = np.float32(1.0 / math.sqrt(segments * (length // 2)))
    return np.concatenate([factor * np.cos(angles), -factor * np.sin(angles)], axis=0).astype(jnp.bfloat16)


def pick_body(owner_ref, records_ref, wanted_ref, sems):
    steps, stations, _ = wanted_ref.shape
    copies = []
    for k in range(steps):
        start = pl.multiple_of(owner_ref[k] * stations, stations)
        copies.append(pltpu.make_async_copy(records_ref.at[pl.ds(start, stations)], wanted_ref.at[k], sems.at[k]))
    for copy in copies:
        copy.start()
    for copy in copies:
        copy.wait()


def pick(owner, records, stations):
    steps = owner.shape[0]
    return pl.pallas_call(
        pick_body,
        out_shape=jax.ShapeDtypeStruct((steps, stations, records.shape[1]), records.dtype),
        in_specs=[pl.BlockSpec(memory_space=pltpu.SMEM), pl.BlockSpec(memory_space=pltpu.HBM)],
        out_specs=pl.BlockSpec(memory_space=pltpu.VMEM),
        scratch_shapes=[pltpu.SemaphoreType.DMA((steps,))],
        compiler_params=pltpu.CompilerParams(vmem_limit_bytes=53 * 2**20),
    )(owner, records)


def band_body(row_ref, out_ref):
    width, height = 2 * LANES, 4 * LANES
    rows = jnp.broadcast_to(row_ref[...], (width, height))
    out_ref[...] = pltpu.roll(rows, 0, 1, stride=1, stride_axis=0).T.astype(out_ref.dtype)


def band_matrix(filter_taps):
    count = filter_taps.shape[0]
    before = LANES - (count - 1) // 2
    row = jnp.pad(filter_taps.astype(jnp.float32), (before, 4 * LANES - before - count))[None]
    return pl.pallas_call(
        band_body,
        out_shape=jax.ShapeDtypeStruct((4 * LANES, 2 * LANES), filter_taps.dtype),
        in_specs=[pl.BlockSpec(memory_space=pltpu.VMEM)],
        out_specs=pl.BlockSpec(memory_space=pltpu.VMEM),
        compiler_params=pltpu.CompilerParams(vmem_limit_bytes=4 * 2**20),
    )(row)


def fetch_body(source_ref, out_ref, sem):
    copy = pltpu.make_async_copy(source_ref, out_ref, sem)
    copy.start()
    copy.wait()


def fetch(matrix):
    return pl.pallas_call(
        fetch_body,
        out_shape=jax.ShapeDtypeStruct(matrix.shape, matrix.dtype),
        in_specs=[pl.BlockSpec(memory_space=pltpu.HBM)],
        out_specs=pl.BlockSpec(memory_space=pltpu.VMEM),
        scratch_shapes=[pltpu.SemaphoreType.DMA],
        compiler_params=pltpu.CompilerParams(vmem_limit_bytes=50 * 2**20),
    )(matrix)


def whiten_body(index_ref, *rest, offsets, rows):
    band_ref, forward_ref, out_ref, padded, filtered = rest[-5:]
    stacks = rest[:-5]
    held = [(o, stacks[k].at[i]) for k, some in enumerate(offsets) for i, o in enumerate(some)]
    stations = padded.shape[1]
    width = stacks[0].shape[-1]
    tiles = NFFT // LANES
    parts = width // LANES
    segments = out_ref.shape[0]
    bins = NFFT // 2
    edge = jnp.zeros((stations, LANES), padded.dtype)
    padded[0] = edge
    padded[segments * tiles + 1] = edge
    for offset, piece in held:
        place = 1 + (index_ref[0] ^ offset) * parts
        for part in range(parts):
            padded[place + part] = piece[:, part * LANES : (part + 1) * LANES]
    for first in range(0, segments, rows // stations):
        some = range(first, first + rows // stations)
        for tile in range(0, tiles, 2):
            window = jnp.concatenate(
                [jnp.concatenate([padded[g * tiles + tile + i] for g in some], axis=0) for i in range(4)], axis=1
            )
            filtered[:, tile * LANES : (tile + 2) * LANES] = jnp.dot(
                window, band_ref[...], preferred_element_type=jnp.float32
            ).astype(jnp.bfloat16)
        spectra = jnp.dot(filtered[...], forward_ref[...], preferred_element_type=jnp.float32)
        real_part, imag_part = spectra[:, :bins], spectra[:, bins:]
        energy = real_part * real_part + imag_part * imag_part
        water_level = jnp.sum(energy, axis=-1, keepdims=True) * (1.0 / bins)
        factor = lax.rsqrt(energy + water_level + 1e-06)
        some = slice(first, first + rows // stations)
        out_ref[some, :, :bins] = (real_part * factor).astype(jnp.bfloat16).reshape(-1, stations, bins)
        out_ref[some, :, bins:] = (imag_part * factor).astype(jnp.bfloat16).reshape(-1, stations, bins)


def whiten(raw, offsets, index, band, forward, rows=128):
    _, stations, width = raw[0].shape
    pieces = sum(stack.shape[0] for stack in raw)
    segments = pieces * width // NFFT
    return pl.pallas_call(
        functools.partial(whiten_body, offsets=offsets, rows=rows),
        out_shape=jax.ShapeDtypeStruct((segments, stations, NFFT), jnp.bfloat16),
        in_specs=[pl.BlockSpec(memory_space=pltpu.SMEM)] + [pl.BlockSpec(memory_space=pltpu.VMEM)] * (len(raw) + 2),
        out_specs=pl.BlockSpec(memory_space=pltpu.VMEM),
        scratch_shapes=[
            pltpu.VMEM((segments * NFFT // LANES + 2, stations, LANES), jnp.bfloat16),
            pltpu.VMEM((rows, NFFT), jnp.bfloat16),
        ],
        compiler_params=pltpu.CompilerParams(vmem_limit_bytes=10 * 2**20),
        cost_estimate=pl.CostEstimate(
            flops=2 * segments * stations * NFFT * (NFFT + 512),
            bytes_accessed=2 * segments * stations * NFFT * 2,
            transcendentals=0,
        ),
    )(index, *raw, band, forward)


def correlate_body(
    mine_ref, order_ref, valid_ref, own_ref, first_ref, second_ref, inverse_ref, out_ref, *rest, group, piece, unroll, pitch
):
    paired, products, cross, ready, sems = rest
    segments, stations, width = own_ref.shape
    steps, block = order_ref.shape
    count = steps * block
    bins = width // 2
    tiles = bins // LANES
    depth = 2 * segments
    half = 2 * stations
    (near, far), (near_out, far_out) = pitch
    mine = mine_ref[0]

    def arrange(g, _):
        for tile in range(tiles):
            real = slice(tile * LANES, (tile + 1) * LANES)
            imag = slice(bins + tile * LANES, bins + (tile + 1) * LANES)
            re, im = own_ref[g, :, real], own_ref[g, :, imag]
            for part in range(2):
                lanes = imag if part else real
                chosen = [first_ref[g, :, lanes], second_ref[g, :, lanes]]
                resident = [im, re] if part else [re, -im]
                stack = jnp.concatenate(resident + chosen if tile % 2 == 0 else chosen + resident, axis=0)
                where = pl.ds((part * segments + g) * near + tile, LANES, stride=far)
                paired[where, :] = stack.T.astype(jnp.float32)
        return 0

    lax.fori_loop(0, segments, arrange, 0, unroll=8)
    low = lax.broadcasted_iota(jnp.int32, (depth, LANES), 1) < half
    column = lax.broadcasted_iota(jnp.int32, (count, tiles * depth), 1)
    even = lax.rem(lax.div(column, depth), 2) == 0
    none = jnp.zeros((), jnp.bfloat16)
    zeros = jnp.zeros((depth, LANES), jnp.bfloat16)

    def multiply(q, _):
        parts = [
            paired[pl.ds(q * far + tile, depth, stride=near), :].astype(jnp.bfloat16) for tile in range(tiles)
        ]
        turned = jnp.concatenate(parts, axis=0).T
        left = jnp.where(even, turned[half:], turned[:half])
        right = []
        for tile in range(tiles):
            kept = jnp.where(low if tile % 2 == 0 else ~low, parts[tile], none)
            blocks = [zeros] * (tiles // 2)
            blocks[tile // 2] = kept
            right.append(jnp.concatenate(blocks, axis=1))
        result = jnp.dot(left, jnp.concatenate(right, axis=0), preferred_element_type=jnp.float32)
        for h in range(tiles // 2):
            products[pl.ds(q * far_out + h, count, stride=near_out), :] = result[:, h * LANES : (h + 1) * LANES]
        return 0

    lax.fori_loop(0, LANES, multiply, 0, unroll=unroll)
    square = (stations, stations)
    diagonal = lax.broadcasted_iota(jnp.int32, square, 0) == lax.broadcasted_iota(jnp.int32, square, 1)
    turns = count // group

    def place(n):
        return lax.div(n, block // group), pl.multiple_of(lax.rem(n, block // group) * group, group)

    def send(n, part):
        step, start = place(n)
        rows = pl.ds(part * piece, piece)
        where = out_ref.at[step, pl.ds(pl.multiple_of(start + part * piece, piece), piece)]
        return pltpu.make_async_copy(ready.at[n, rows], where, sems.at[n, part])

    def finish(n, _):
        step, start = place(n)
        for j in range(group):
            row = (step ^ mine) * block + order_ref[step, start + j]
            for h in range(tiles // 2):
                turned = products[pl.ds(row * near_out + h, LANES, stride=far_out), :].astype(jnp.bfloat16).T
                for tile in range(2):
                    for part in range(2):
                        at = (2 * tile + part) * stations
                        lane = part * bins + (2 * h + tile) * LANES
                        cross[j * stations : (j + 1) * stations, lane : lane + LANES] = turned[at : at + stations]
        valid = valid_ref[step, pl.ds(start, group), :].astype(jnp.float32)
        for part in range(group // piece):
            lagged = jnp.dot(
                cross[part * piece * stations : (part + 1) * piece * stations],
                inverse_ref[...],
                preferred_element_type=jnp.float32,
            )
            for i in range(piece):
                j = part * piece + i
                kept = jnp.sum(
                    jnp.where(diagonal, jnp.broadcast_to(valid[j : j + 1], square), 0.0), axis=1, keepdims=True
                )
                ready[n, j] = lagged[i * stations : (i + 1) * stations] * kept
            send(n, part).start()
        return 0

    lax.fori_loop(0, turns, finish, 0)
    for n in range(turns):
        for part in range(group // piece):
            send(n, part).wait()


def correlate(mine, order, valid, own, first, second, inverse):
    segments, stations, width = own.shape
    steps, block = order.shape
    count = steps * block
    lags = inverse.shape[1]
    tiles = width // 2 // LANES
    depth = 2 * segments
    assert steps == 2 and tiles * depth == LANES and 2 * stations == count and 4 * stations == LANES
    group = block
    near, near_out = tiles + 1, tiles // 2 + 1
    pitch = (near, near * depth + 1), (near_out, near_out * count + 1)
    vmem, smem = pl.BlockSpec(memory_space=pltpu.VMEM), pl.BlockSpec(memory_space=pltpu.SMEM)
    return pl.pallas_call(
        functools.partial(correlate_body, group=group, piece=PIECE, unroll=64, pitch=pitch),
        out_shape=jax.ShapeDtypeStruct((steps, block, stations, lags), jnp.float32),
        in_specs=[smem] * 2 + [vmem] * 5,
        out_specs=pl.BlockSpec(memory_space=pl.ANY),
        scratch_shapes=[
            pltpu.VMEM((LANES * pitch[0][1], LANES), jnp.float32),
            pltpu.VMEM((LANES * pitch[1][1], LANES), jnp.float32),
            pltpu.VMEM((group * stations, width), jnp.bfloat16),
            pltpu.VMEM((count // group, group, stations, lags), jnp.float32),
            pltpu.SemaphoreType.DMA((count // group, group // PIECE)),
        ],
        compiler_params=pltpu.CompilerParams(vmem_limit_bytes=33 * 2**20),
        cost_estimate=pl.CostEstimate(
            flops=10**10,
            bytes_accessed=(own.size + first.size + second.size) * 2 + count * stations * lags * 4,
            transcendentals=0,
        ),
    )(mine, order, valid, own, first, second, inverse)


def swap(block, axis, distance):
    count = lax.axis_size(axis)
    return lax.ppermute(block, axis, [(i, i ^ distance) for i in range(count)])


def local(records, filter_taps, ref_owner, reference_station_order, pair_valid):
    axis = "sta"
    devices = lax.axis_size(axis)
    index = lax.axis_index(axis).astype(jnp.int32)
    stations = records.shape[0] // devices
    width = records.shape[1]

    wanted = pick(ref_owner, records, stations)
    own_piece = wanted[None]
    quarter = devices // 4
    crossed = [swap(own_piece, axis, j * quarter) for j in range(1, 4)]
    chains = {
        "near": (jnp.concatenate([own_piece, crossed[0]], axis=0), [0, quarter]),
        "far": (jnp.concatenate(crossed[1:], axis=0), [2 * quarter, 3 * quarter]),
    }
    distance, stage = devices // 8, 0
    while distance > 1:
        for name, (block, offsets) in chains.items():
            block = jnp.concatenate([block, swap(block, axis, distance)], axis=0)
            chains[name] = block, offsets + [distance | o for o in offsets]
        distance //= 2
        stage += 1
    mine = lax.rem(index, 2)
    pieces, offsets = [], []
    for (block, some) in chains.values():
        pieces.append(lax.dynamic_index_in_dim(block, mine, 1, keepdims=False))
        pieces.append(swap(lax.dynamic_index_in_dim(block, 1 - mine, 1, keepdims=False), axis, 1))
        offsets += [some, [o | 1 for o in some]]

    rows = lax.all_to_all(records.reshape(devices, stations, width), axis, split_axis=0, concat_axis=0)

    band = band_matrix(filter_taps)
    forward = fetch(jnp.asarray(forward_matrix(NFFT)))
    inverse = jnp.asarray(inverse_transform_matrix(NFFT, LAGS, devices * width // NFFT))
    first = whiten(pieces, offsets, index[None], band, forward)
    second = swap(first, axis, 1)
    own = whiten([rows], [list(range(devices))], jnp.zeros((1,), jnp.int32), band, forward)
    return correlate(mine[None], reference_station_order, pair_valid, own, first, second, inverse)


def solution(mesh):
    placed = (P("win", "sta"), P(), P("win"), P("win", None), P("win", None, "sta"))
    return jax.shard_map(local, mesh=mesh, in_specs=placed, out_specs=P("win", None, "sta", None), check_vma=False)
```

```python
import functools
import math

import jax
import jax.numpy as jnp
import numpy as np
from jax import lax
from jax.experimental import pallas as pl
from jax.experimental.pallas import tpu as pltpu
from jax.sharding import PartitionSpec as P


NFFT = 1024
PIECE = 8
LAGS = 256
LANES = 128


def forward_matrix(length):
    time_index = np.arange(length)[:, None]
    bin_index = np.arange(length // 2)[None, :]
    angles = (time_index * bin_index % length).astype(np.float32) * np.float32(2.0 * math.pi / length)
    return np.concatenate([np.cos(angles), -np.sin(angles)], axis=1).astype(jnp.bfloat16)


def inverse_transform_matrix(length, lag_count, segments):
    bin_index = np.arange(length // 2)[:, None]
    shifts = np.arange(lag_count)[None, :] - lag_count // 2
    angles = (bin_index * shifts % length).astype(np.float32) * np.float32(2.0 * math.pi / length)
    factor = np.float32(1.0 / math.sqrt(segments * (length // 2)))
    return np.concatenate([factor * np.cos(angles), -factor * np.sin(angles)], axis=0).astype(jnp.bfloat16)


def pick_body(owner_ref, records_ref, wanted_ref, sems):
    steps, stations, _ = wanted_ref.shape
    copies = []
    for k in range(steps):
        start = pl.multiple_of(owner_ref[k] * stations, stations)
        copies.append(pltpu.make_async_copy(records_ref.at[pl.ds(start, stations)], wanted_ref.at[k], sems.at[k]))
    for copy in copies:
        copy.start()
    for copy in copies:
        copy.wait()


def pick(owner, records, stations):
    steps = owner.shape[0]
    return pl.pallas_call(
        pick_body,
        out_shape=jax.ShapeDtypeStruct((steps, stations, records.shape[1]), records.dtype),
        in_specs=[pl.BlockSpec(memory_space=pltpu.SMEM), pl.BlockSpec(memory_space=pltpu.HBM)],
        out_specs=pl.BlockSpec(memory_space=pltpu.VMEM),
        scratch_shapes=[pltpu.SemaphoreType.DMA((steps,))],
        compiler_params=pltpu.CompilerParams(vmem_limit_bytes=53 * 2**20),
    )(owner, records)


def band_body(row_ref, out_ref):
    width, height = 2 * LANES, 4 * LANES
    rows = jnp.broadcast_to(row_ref[...], (width, height))
    out_ref[...] = pltpu.roll(rows, 0, 1, stride=1, stride_axis=0).T.astype(out_ref.dtype)


def band_matrix(filter_taps):
    count = filter_taps.shape[0]
    before = LANES - (count - 1) // 2
    row = jnp.pad(filter_taps.astype(jnp.float32), (before, 4 * LANES - before - count))[None]
    return pl.pallas_call(
        band_body,
        out_shape=jax.ShapeDtypeStruct((4 * LANES, 2 * LANES), filter_taps.dtype),
        in_specs=[pl.BlockSpec(memory_space=pltpu.VMEM)],
        out_specs=pl.BlockSpec(memory_space=pltpu.VMEM),
        compiler_params=pltpu.CompilerParams(vmem_limit_bytes=4 * 2**20),
    )(row)


def fetch_body(source_ref, out_ref, sem):
    copy = pltpu.make_async_copy(source_ref, out_ref, sem)
    copy.start()
    copy.wait()


def fetch(matrix):
    return pl.pallas_call(
        fetch_body,
        out_shape=jax.ShapeDtypeStruct(matrix.shape, matrix.dtype),
        in_specs=[pl.BlockSpec(memory_space=pltpu.HBM)],
        out_specs=pl.BlockSpec(memory_space=pltpu.VMEM),
        scratch_shapes=[pltpu.SemaphoreType.DMA],
        compiler_params=pltpu.CompilerParams(vmem_limit_bytes=50 * 2**20),
    )(matrix)


def whiten_body(index_ref, *rest, offsets, rows):
    band_ref, forward_ref, out_ref, padded, filtered = rest[-5:]
    stacks = rest[:-5]
    held = [(o, stacks[k].at[i]) for k, some in enumerate(offsets) for i, o in enumerate(some)]
    stations = padded.shape[1]
    width = stacks[0].shape[-1]
    tiles = NFFT // LANES
    parts = width // LANES
    segments = out_ref.shape[0]
    bins = NFFT // 2
    edge = jnp.zeros((stations, LANES), padded.dtype)
    padded[0] = edge
    padded[segments * tiles + 1] = edge
    for offset, piece in held:
        place = 1 + (index_ref[0] ^ offset) * parts
        for part in range(parts):
            padded[place + part] = piece[:, part * LANES : (part + 1) * LANES]
    for first in range(0, segments, rows // stations):
        some = range(first, first + rows // stations)
        for tile in range(0, tiles, 2):
            window = jnp.concatenate(
                [jnp.concatenate([padded[g * tiles + tile + i] for g in some], axis=0) for i in range(4)], axis=1
            )
            filtered[:, tile * LANES : (tile + 2) * LANES] = jnp.dot(
                window, band_ref[...], preferred_element_type=jnp.float32
            ).astype(jnp.bfloat16)
        spectra = jnp.dot(filtered[...], forward_ref[...], preferred_element_type=jnp.float32)
        real_part, imag_part = spectra[:, :bins], spectra[:, bins:]
        energy = real_part * real_part + imag_part * imag_part
        water_level = jnp.sum(energy, axis=-1, keepdims=True) * (1.0 / bins)
        factor = lax.rsqrt(energy + water_level + 1e-06)
        some = slice(first, first + rows // stations)
        out_ref[some, :, :bins] = (real_part * factor).astype(jnp.bfloat16).reshape(-1, stations, bins)
        out_ref[some, :, bins:] = (imag_part * factor).astype(jnp.bfloat16).reshape(-1, stations, bins)


def whiten(raw, offsets, index, band, forward, rows=128):
    _, stations, width = raw[0].shape
    pieces = sum(stack.shape[0] for stack in raw)
    segments = pieces * width // NFFT
    return pl.pallas_call(
        functools.partial(whiten_body, offsets=offsets, rows=rows),
        out_shape=jax.ShapeDtypeStruct((segments, stations, NFFT), jnp.bfloat16),
        in_specs=[pl.BlockSpec(memory_space=pltpu.SMEM)] + [pl.BlockSpec(memory_space=pltpu.VMEM)] * (len(raw) + 2),
        out_specs=pl.BlockSpec(memory_space=pltpu.VMEM),
        scratch_shapes=[
            pltpu.VMEM((segments * NFFT // LANES + 2, stations, LANES), jnp.bfloat16),
            pltpu.VMEM((rows, NFFT), jnp.bfloat16),
        ],
        compiler_params=pltpu.CompilerParams(vmem_limit_bytes=10 * 2**20),
        cost_estimate=pl.CostEstimate(
            flops=2 * segments * stations * NFFT * (NFFT + 512),
            bytes_accessed=2 * segments * stations * NFFT * 2,
            transcendentals=0,
        ),
    )(index, *raw, band, forward)


def correlate_body(
    mine_ref, order_ref, valid_ref, own_ref, first_ref, second_ref, inverse_ref, out_ref, *rest, group, piece, unroll, pitch
):
    paired, products, cross, ready, sems = rest
    segments, stations, width = own_ref.shape
    steps, block = order_ref.shape
    count = steps * block
    bins = width // 2
    tiles = bins // LANES
    depth = 2 * segments
    half = 2 * stations
    (near, far), (near_out, far_out) = pitch
    mine = mine_ref[0]

    def arrange(g, _):
        for tile in range(tiles):
            real = slice(tile * LANES, (tile + 1) * LANES)
            imag = slice(bins + tile * LANES, bins + (tile + 1) * LANES)
            re, im = own_ref[g, :, real], own_ref[g, :, imag]
            for part in range(2):
                lanes = imag if part else real
                chosen = [first_ref[g, :, lanes], second_ref[g, :, lanes]]
                resident = [im, re] if part else [re, -im]
                stack = jnp.concatenate(resident + chosen if tile % 2 == 0 else chosen + resident, axis=0)
                where = pl.ds((part * segments + g) * near + tile, LANES, stride=far)
                paired[where, :] = stack.T.astype(jnp.float32)
        return 0

    lax.fori_loop(0, segments, arrange, 0, unroll=8)
    low = lax.broadcasted_iota(jnp.int32, (depth, LANES), 1) < half
    column = lax.broadcasted_iota(jnp.int32, (count, tiles * depth), 1)
    even = lax.rem(lax.div(column, depth), 2) == 0
    none = jnp.zeros((), jnp.bfloat16)
    zeros = jnp.zeros((depth, LANES), jnp.bfloat16)

    def multiply(q, _):
        parts = [
            paired[pl.ds(q * far + tile, depth, stride=near), :].astype(jnp.bfloat16) for tile in range(tiles)
        ]
        turned = jnp.concatenate(parts, axis=0).T
        left = jnp.where(even, turned[half:], turned[:half])
        right = []
        for tile in range(tiles):
            kept = jnp.where(low if tile % 2 == 0 else ~low, parts[tile], none)
            blocks = [zeros] * (tiles // 2)
            blocks[tile // 2] = kept
            right.append(jnp.concatenate(blocks, axis=1))
        result = jnp.dot(left, jnp.concatenate(right, axis=0), preferred_element_type=jnp.float32)
        for h in range(tiles // 2):
            products[pl.ds(q * far_out + h, count, stride=near_out), :] = result[:, h * LANES : (h + 1) * LANES]
        return 0

    lax.fori_loop(0, LANES, multiply, 0, unroll=unroll)
    square = (stations, stations)
    diagonal = lax.broadcasted_iota(jnp.int32, square, 0) == lax.broadcasted_iota(jnp.int32, square, 1)
    turns = count // group

    def place(n):
        return lax.div(n, block // group), pl.multiple_of(lax.rem(n, block // group) * group, group)

    def send(n, part):
        step, start = place(n)
        rows = pl.ds(part * piece, piece)
        where = out_ref.at[step, pl.ds(pl.multiple_of(start + part * piece, piece), piece)]
        return pltpu.make_async_copy(ready.at[n, rows], where, sems.at[n, part])

    def finish(n, _):
        step, start = place(n)
        for j in range(group):
            row = (step ^ mine) * block + order_ref[step, start + j]
            for h in range(tiles // 2):
                turned = products[pl.ds(row * near_out + h, LANES, stride=far_out), :].astype(jnp.bfloat16).T
                for tile in range(2):
                    for part in range(2):
                        at = (2 * tile + part) * stations
                        lane = part * bins + (2 * h + tile) * LANES
                        cross[j * stations : (j + 1) * stations, lane : lane + LANES] = turned[at : at + stations]
        valid = valid_ref[step, pl.ds(start, group), :].astype(jnp.float32)
        for part in range(group // piece):
            lagged = jnp.dot(
                cross[part * piece * stations : (part + 1) * piece * stations],
                inverse_ref[...],
                preferred_element_type=jnp.float32,
            )
            for i in range(piece):
                j = part * piece + i
                kept = jnp.sum(
                    jnp.where(diagonal, jnp.broadcast_to(valid[j : j + 1], square), 0.0), axis=1, keepdims=True
                )
                ready[n, j] = lagged[i * stations : (i + 1) * stations] * kept
            send(n, part).start()
        return 0

    lax.fori_loop(0, turns, finish, 0)
    for n in range(turns):
        for part in range(group // piece):
            send(n, part).wait()


def correlate(mine, order, valid, own, first, second, inverse):
    segments, stations, width = own.shape
    steps, block = order.shape
    count = steps * block
    lags = inverse.shape[1]
    tiles = width // 2 // LANES
    depth = 2 * segments
    assert steps == 2 and tiles * depth == LANES and 2 * stations == count and 4 * stations == LANES
    group = block
    near, near_out = tiles + 1, tiles // 2 + 1
    pitch = (near, near * depth + 1), (near_out, near_out * count + 1)
    vmem, smem = pl.BlockSpec(memory_space=pltpu.VMEM), pl.BlockSpec(memory_space=pltpu.SMEM)
    return pl.pallas_call(
        functools.partial(correlate_body, group=group, piece=PIECE, unroll=64, pitch=pitch),
        out_shape=jax.ShapeDtypeStruct((steps, block, stations, lags), jnp.float32),
        in_specs=[smem] * 2 + [vmem] * 5,
        out_specs=pl.BlockSpec(memory_space=pl.ANY),
        scratch_shapes=[
            pltpu.VMEM((LANES * pitch[0][1], LANES), jnp.float32),
            pltpu.VMEM((LANES * pitch[1][1], LANES), jnp.float32),
            pltpu.VMEM((group * stations, width), jnp.bfloat16),
            pltpu.VMEM((count // group, group, stations, lags), jnp.float32),
            pltpu.SemaphoreType.DMA((count // group, group // PIECE)),
        ],
        compiler_params=pltpu.CompilerParams(vmem_limit_bytes=33 * 2**20),
        cost_estimate=pl.CostEstimate(
            flops=10**10,
            bytes_accessed=(own.size + first.size + second.size) * 2 + count * stations * lags * 4,
            transcendentals=0,
        ),
    )(mine, order, valid, own, first, second, inverse)


def swap(block, axis, distance):
    count = lax.axis_size(axis)
    return lax.ppermute(block, axis, [(i, i ^ distance) for i in range(count)])


def local(records, filter_taps, ref_owner, reference_station_order, pair_valid):
    axis = "sta"
    devices = lax.axis_size(axis)
    index = lax.axis_index(axis).astype(jnp.int32)
    stations = records.shape[0] // devices
    width = records.shape[1]

    wanted = pick(ref_owner, records, stations)
    own_piece = wanted[None]
    quarter = devices // 4
    crossed = [swap(own_piece, axis, j * quarter) for j in range(1, 4)]
    own_passed = swap(own_piece, axis, quarter // 2)
    chains = {
        "near": (jnp.concatenate([own_piece, crossed[0]], axis=0), [0, quarter]),
        "far": (jnp.concatenate(crossed[1:], axis=0), [2 * quarter, 3 * quarter]),
    }
    distance, stage = devices // 8, 0
    while distance > 1:
        for name, (block, offsets) in chains.items():
            if name == "near" and stage == 0:
                passed = [own_passed, swap(crossed[0], axis, distance)]
            else:
                passed = [swap(block, axis, distance)]
            block = jnp.concatenate([block, *passed], axis=0)
            chains[name] = block, offsets + [distance | o for o in offsets]
        distance //= 2
        stage += 1
    mine = lax.rem(index, 2)
    pieces, offsets = [], []
    for (block, some) in chains.values():
        pieces.append(lax.dynamic_index_in_dim(block, mine, 1, keepdims=False))
        pieces.append(swap(lax.dynamic_index_in_dim(block, 1 - mine, 1, keepdims=False), axis, 1))
        offsets += [some, [o | 1 for o in some]]

    rows = lax.all_to_all(records.reshape(devices, stations, width), axis, split_axis=0, concat_axis=0)

    band = band_matrix(filter_taps)
    forward = fetch(jnp.asarray(forward_matrix(NFFT)))
    inverse = jnp.asarray(inverse_transform_matrix(NFFT, LAGS, devices * width // NFFT))
    first = whiten(pieces, offsets, index[None], band, forward)
    second = swap(first, axis, 1)
    own = whiten([rows], [list(range(devices))], jnp.zeros((1,), jnp.int32), band, forward)
    return correlate(mine[None], reference_station_order, pair_valid, own, first, second, inverse)


def solution(mesh):
    placed = (P("win", "sta"), P(), P("win"), P("win", None), P("win", None, "sta"))
    return jax.shard_map(local, mesh=mesh, in_specs=placed, out_specs=P("win", None, "sta", None), check_vma=False)
```
